128 devices in a mesh: ax: 8 (over y, z_lo), az: 16 (over z_hi, x, core).
Axes of the slice: x: 4, y: 4, z: 4 (z_hi: 2, z_lo: 2; z = z_hi * 2 + z_lo), core: 2. Of those that a mesh axis runs over, the one named last changes fastest.
Arguments:
- saved_flow: float32 [3, 256, 64, 1024], P(None, 'az', None, 'ax'), may hold values from -6 to 6
- saved_adjoint: float32 [3, 256, 64, 1024], P(None, 'az', None, 'ax'), may hold values from -6 to 6
- tangent: float32 [3, 256, 64, 1024], P(None, 'az', None, 'ax'), may hold values from -6 to 6
- second_adjoint: float32 [3, 256, 64, 1024], P(None, 'az', None, 'ax'), may hold values from -6 to 6
- radial_rate: float32 [64], replicated, may hold values from 1 to 100
Outputs:
- tangent_next: float32 [3, 256, 64, 1024], P(None, 'az', None, 'ax')
- second_next: float32 [3, 256, 64, 1024], P(None, 'az', None, 'ax')
The draws below stay inside these ranges and needn't reach their ends.
All inputs are finite; a program needn't handle non-finite values.
Results may differ from the reference program's by a relative error of at most 0.00005.
Values sent between devices are 32-bit elements; how exact they have to be, the bound alone decides.
No kernel may reach another device: no remote copies, remote signals or barrier semaphores. Data moves between devices by JAX's collectives and lax.ppermute only.
A program may use at most 128 MiB of HBM per device.

```python
import math
import jax
import jax.numpy as jnp
from jax import lax

NR = 64
MA = 256
KX = 1024


def block_scale(stream_key, dims, cuts, least, largest):
    loudness, own = 1.0, jax.random.fold_in(stream_key, 6)
    for axis_at, blocks in cuts:
        steps = jnp.exp(jax.random.uniform(jax.random.fold_in(own, axis_at), (blocks,), jnp.float32, least / len(cuts), largest / len(cuts)))
        loudness = loudness * jnp.repeat(steps, dims[axis_at] // blocks).reshape([-1 if axis == axis_at else 1 for axis in range(len(dims))])
    return loudness


def bell_draw(rng, extent, width, most, cuts=(), kind=jnp.bfloat16):
    array = width * jax.random.normal(rng, extent, jnp.float32)
    if cuts:
        array = array * block_scale(rng, extent, cuts, -0.22, 0.18)
    return jnp.clip(array, -most, most).astype(kind)


def setup_inputs(seed: int = 0) -> dict:
    keys = jax.random.split(jax.random.key(seed), 6)
    saved_flow = bell_draw(keys[0], (3, MA, NR, KX), 1.0, 6.0, ((1, 16), (3, 8)), jnp.float32)
    saved_adjoint = bell_draw(keys[1], (3, MA, NR, KX), 1.0, 6.0, ((1, 16), (3, 8)), jnp.float32)
    tangent = bell_draw(keys[2], (3, MA, NR, KX), 1.0, 6.0, ((1, 16), (3, 8)), jnp.float32)
    second_adjoint = bell_draw(keys[3], (3, MA, NR, KX), 1.0, 6.0, ((1, 16), (3, 8)), jnp.float32)
    radial_rate = jnp.clip(jnp.exp(jax.random.uniform(keys[4], (NR,), jnp.float32, math.log(1.0), math.log(100.0))), 1.0, 100.0)
    return dict(saved_flow=saved_flow, saved_adjoint=saved_adjoint, tangent=tangent, second_adjoint=second_adjoint, radial_rate=radial_rate)


time_step = 0.1
viscosity = 0.005
axial_unit = 2.0 * math.pi / 20.0

def radial_table(count):
    points = jnp.arange(count, dtype=jnp.int32)[:, None]
    orders = jnp.arange(count, dtype=jnp.int32)[None, :]
    phases = orders * (2 * points + 1) % (4 * count)
    values = jnp.cos(phases.astype(jnp.float32) * (math.pi / (2.0 * count)))
    scales = jnp.where(orders == 0, math.sqrt(1.0 / count), math.sqrt(2.0 / count))
    return (values * scales).astype(jnp.float32)

def hartley(field, axis):
    length = field.shape[axis]
    spectrum = jnp.fft.fft(field, axis=axis)
    return (spectrum.real - spectrum.imag) / math.sqrt(length)

def to_physical(field, table):
    grid = jnp.einsum('jr,cmrk->cmjk', table, field, precision=lax.Precision.HIGHEST)
    return hartley(hartley(grid, 1), 3)

def to_spectral(field, table):
    spectral = hartley(hartley(field, 3), 1)
    return jnp.einsum('jr,cmjk->cmrk', table, spectral, precision=lax.Precision.HIGHEST)

def damping(radial_rate):
    azimuth = jnp.arange(MA, dtype=jnp.int32)
    wave_azimuth = jnp.minimum(azimuth, MA - azimuth).astype(jnp.float32)
    axial = jnp.arange(KX, dtype=jnp.int32)
    wave_axial = jnp.minimum(axial, KX - axial).astype(jnp.float32) * axial_unit
    total = radial_rate[None, :, None] + (wave_azimuth ** 2)[:, None, None] + (wave_axial ** 2)[None, None, :]
    return 1.0 + viscosity * total

def reference(saved_flow, saved_adjoint, tangent, second_adjoint, radial_rate):
    table = radial_table(NR)
    flow = to_physical(saved_flow, table)
    adjoint = to_physical(saved_adjoint, table)
    tang = to_physical(tangent, table)
    second = to_physical(second_adjoint, table)
    flow_sum = lax.optimization_barrier(jnp.sum(flow, axis=0))[None]
    adjoint_sum = lax.optimization_barrier(jnp.sum(adjoint, axis=0))[None]
    tang_sum = lax.optimization_barrier(jnp.sum(tang, axis=0))[None]
    second_sum = lax.optimization_barrier(jnp.sum(second, axis=0))[None]
    tangent_rhs = flow * tang_sum + tang * flow_sum
    second_rhs = flow * second_sum + second * flow_sum + adjoint * tang_sum + tang * adjoint_sum
    tangent_term = to_spectral(tangent_rhs, table)
    second_term = to_spectral(second_rhs, table)
    denom = damping(radial_rate)[None]
    tangent_next = (tangent + time_step * tangent_term) / denom
    second_next = (second_adjoint + time_step * second_term) / denom
    return (tangent_next, second_next)
```

```python
import math

import jax
import jax.numpy as jnp
import numpy as np
from jax import lax
from jax.experimental import pallas as pl
from jax.experimental.pallas import tpu as pltpu
from jax.sharding import PartitionSpec as P

time_step = 0.1
viscosity = 0.005
axial_unit = 2.0 * math.pi / 20.0
F32 = jnp.float32
BF16 = jnp.bfloat16


def radial_table(count):
    points = np.arange(count)[:, None]
    orders = np.arange(count)[None, :]
    phases = orders * (2 * points + 1) % (4 * count)
    scales = np.where(orders == 0, math.sqrt(1.0 / count), math.sqrt(2.0 / count))
    return np.cos(phases * (math.pi / (2.0 * count))) * scales


def hartley_table(rows, cols, length):
    angles = (rows[:, None] * cols[None, :] % length) * (2.0 * math.pi / length)
    return (np.cos(angles) + np.sin(angles)) / math.sqrt(length)


def halves(table):
    table = np.asarray(table, np.float32)
    high = table.astype(BF16)
    low = (table - high.astype(np.float32)).astype(BF16)
    return np.stack((high, low))


def split(x):
    high = x.astype(BF16)
    return high, (x - high.astype(F32)).astype(BF16)


def table_dot(table, x):
    high, low = split(x)
    left = jnp.concatenate((table[0], table[0], table[1]), axis=1)
    right = jnp.concatenate((high, low, high), axis=0)
    return jnp.dot(left, right, preferred_element_type=F32)


def dot_table(x, table, turned):
    high, low = split(x)
    left = jnp.concatenate((high, low, high), axis=1)
    right = jnp.concatenate((table[0], table[0], table[1]), axis=1 if turned else 0)
    return lax.dot_general(
        left, right, (((1,), (1 if turned else 0,)), ((), ())), preferred_element_type=F32
    )


def spread_kernel(first_ref, second_ref, wide_ref, out_ref, table_ref):
    radial = wide_ref.shape[0]
    rows = radial * 8
    lane = lax.broadcasted_iota(jnp.int32, (8, rows), 1) // radial
    keep = lane == lax.broadcasted_iota(jnp.int32, (8, rows), 0)
    for j in range(radial):
        block = jnp.where(keep, jnp.broadcast_to(wide_ref[j : j + 1, :], (8, rows)), 0.0)
        high, low = split(block)
        table_ref[0, 8 * j : 8 * j + 8, :] = high
        table_ref[1, 8 * j : 8 * j + 8, :] = low
    table = (table_ref[0], table_ref[1])

    def step(index, _):
        c, group = index // 2, index % 2
        start = pl.multiple_of(group * 8, 8)
        x = jnp.concatenate(
            [ref[c, pl.ds(start, 8)].reshape(rows, 128) for ref in (first_ref, second_ref)], axis=1
        )
        y = table_dot(table, x)
        for core in range(2):
            out_ref[:, core, c, pl.ds(start, 8), :] = y[:, 128 * core : 128 * core + 128].reshape(
                radial, 8, 128
            )
        return _

    lax.fori_loop(0, 6, step, 0)


def forward_kernel(recv_ref, azimuth_ref, even_ref, odd_ref, out_ref):
    axial_parts, azimuth_parts, components = recv_ref.shape[:3]
    azimuth_count = azimuth_ref.shape[1]
    half = even_ref.shape[1]
    azimuth = (azimuth_ref[0], azimuth_ref[1])
    even = (even_ref[0], even_ref[1])
    odd = (odd_ref[0], odd_ref[1])

    def step(c, _):
        x = jnp.concatenate(
            [recv_ref[a, :, c].reshape(azimuth_count, 128) for a in range(axial_parts)], axis=1
        )
        y = table_dot(azimuth, x)
        out_ref[c, :, :half] = dot_table(y[:, :half] + y[:, half:], even, False)
        out_ref[c, :, half:] = dot_table(y[:, :half] - y[:, half:], odd, False)
        return _

    lax.fori_loop(0, components, step, 0)


def inverse(c, rhs, azimuth, even, odd, send_ref):
    half = even[0].shape[0]
    z = table_dot(azimuth, rhs)
    e = dot_table(z[:, :half], even, False)
    o = dot_table(z[:, half:], odd, True)
    for side, y in enumerate((e + o, e - o)):
        for a in range(4):
            send_ref[4 * side + a, :, c] = y[:, 128 * a : 128 * a + 128].reshape(16, 8, 128)


def total(ref):
    return ref[0] + ref[1] + ref[2]


def first_product_kernel(own_ref, other_ref, azimuth_ref, even_ref, odd_ref, send_ref, sums_ref):
    core = lax.axis_index("az") % 2
    azimuth = (azimuth_ref[core, 0], azimuth_ref[core, 1])
    even = (even_ref[0], even_ref[1])
    odd = (odd_ref[0], odd_ref[1])
    sums_ref[0] = total(own_ref)
    sums_ref[1] = total(other_ref)

    def step(c, _):
        rhs = own_ref[c] * sums_ref[1] + other_ref[c] * sums_ref[0]
        inverse(c, rhs, azimuth, even, odd, send_ref)
        return _

    lax.fori_loop(0, 3, step, 0)


def second_product_kernel(
    own_ref, other_ref, own2_ref, other2_ref, azimuth_ref, even_ref, odd_ref, send_ref, sums_ref
):
    core = lax.axis_index("az") % 2
    azimuth = (azimuth_ref[core, 0], azimuth_ref[core, 1])
    even = (even_ref[0], even_ref[1])
    odd = (odd_ref[0], odd_ref[1])
    for i, ref in enumerate((own_ref, other_ref, own2_ref, other2_ref)):
        sums_ref[i] = total(ref)

    def step(c, _):
        rhs = own_ref[c] * sums_ref[2] + own2_ref[c] * sums_ref[0]
        rhs = rhs + (other_ref[c] * sums_ref[3] + other2_ref[c] * sums_ref[1])
        inverse(c, rhs, azimuth, even, odd, send_ref)
        return _

    lax.fori_loop(0, 3, step, 0)


def gather_kernel(recv_ref, field_ref, rate_ref, tall_ref, out_ref, table_ref):
    radial = tall_ref.shape[0]
    rows = radial * 8
    lane = lax.broadcasted_iota(jnp.int32, (radial, rows), 1) % 8
    for m in range(8):
        high, low = split(jnp.where(lane == m, tall_ref[...], 0.0))
        table_ref[0, radial * m : radial * m + radial, :] = high
        table_ref[1, radial * m : radial * m + radial, :] = low
    table = (table_ref[0], table_ref[1])
    azimuth_count, axial_count = 256, 1024
    axial = lax.axis_index("ax") * 128 + lax.broadcasted_iota(jnp.int32, (1, 128), 1)
    wave = jnp.minimum(axial, axial_count - axial).astype(F32) * axial_unit
    base = rate_ref[...] + wave * wave

    def step(c, _):
        x = jnp.concatenate([recv_ref[:, core, c].reshape(rows, 128) for core in range(2)], axis=1)
        y = table_dot(table, x)
        for core in range(2):
            for i in range(8):
                m = 8 * core + i
                azimuth = lax.axis_index("az") * 16 + m
                wave_azimuth = jnp.minimum(azimuth, azimuth_count - azimuth).astype(F32)
                denom = 1.0 + viscosity * (base + wave_azimuth * wave_azimuth)
                term = y[radial * i : radial * i + radial, 128 * core : 128 * core + 128]
                out_ref[c, m] = (field_ref[c, m] + time_step * term) / denom
        return _

    lax.fori_loop(0, 3, step, 0)


def call(kernel, shape, *args, scratch=()):
    return pl.pallas_call(
        kernel,
        out_shape=jax.ShapeDtypeStruct(shape, F32),
        in_specs=[pl.BlockSpec(memory_space=pltpu.VMEM)] * len(args),
        out_specs=pl.BlockSpec(memory_space=pltpu.VMEM),
        scratch_shapes=list(scratch),
        compiler_params=pltpu.CompilerParams(vmem_limit_bytes=60 * 1024 * 1024),
    )(*args)


def body(saved_flow, saved_adjoint, tangent, second_adjoint, radial_rate):
    radial = radial_table(64)
    wide = np.tile(radial, (1, 8)).astype(np.float32)
    tall = np.repeat(radial.T, 8, axis=1).astype(np.float32)
    order = np.arange(256)
    azimuth = halves(hartley_table(order, order, 256))
    kept = [[16 * a + 8 * s + i for a in range(16) for i in range(8)] for s in range(2)]
    azimuth_back = np.stack([halves(hartley_table(np.array(rows), order, 256)) for rows in kept])
    line = np.arange(512)
    even = halves(hartley_table(line, 2 * line, 1024))
    odd = halves(hartley_table(line, 2 * line + 1, 1024))
    rate = jnp.broadcast_to(radial_rate[:, None], (64, 128))
    pairs = [(i, i ^ 1) for i in range(16)]
    table_scratch = (pltpu.VMEM((2, 512, 512), BF16),)

    def sums(count):
        return (pltpu.VMEM((count, 256, 1024), F32),)

    def spread(first, second):
        return call(spread_kernel, (64, 2, 3, 16, 128), first, second, wide, scratch=table_scratch)

    def whole(x):
        x = x.reshape((128,) + x.shape[2:])
        return lax.all_to_all(x, ("ax", "az"), 0, 0, tiled=True)

    def forward(x):
        return call(forward_kernel, (3, 256, 1024), x.reshape(8, 16, 3, 16, 128), azimuth, even, odd)

    def gather(x, field):
        return call(
            gather_kernel,
            (3, 16, 64, 128),
            x.reshape(64, 2, 3, 8, 128),
            field,
            rate,
            tall,
            scratch=table_scratch,
        )

    back = (8, 16, 3, 8, 128)
    first = whole(spread(saved_flow, tangent))
    second = whole(spread(second_adjoint, saved_adjoint))
    own = forward(first)
    other = lax.ppermute(own, "az", pairs)
    tangent_send = call(
        first_product_kernel, back, own, other, azimuth_back, even, odd, scratch=sums(2)
    )
    own2 = forward(second)
    other2 = lax.ppermute(own2, "az", pairs)
    second_send = call(
        second_product_kernel,
        back,
        own,
        other,
        own2,
        other2,
        azimuth_back,
        even,
        odd,
        scratch=sums(4),
    )
    tangent_next = gather(whole(tangent_send), tangent)
    second_next = gather(whole(second_send), second_adjoint)
    return (tangent_next, second_next)


def solution(mesh):
    spec = P(None, "az", None, "ax")
    return jax.shard_map(
        body, mesh=mesh, in_specs=(spec,) * 4 + (P(),), out_specs=(spec, spec), check_vma=False
    )
```

```python
import math

import jax
import jax.numpy as jnp
import numpy as np
from jax import lax
from jax.experimental import pallas as pl
from jax.experimental.pallas import tpu as pltpu
from jax.sharding import PartitionSpec as P

time_step = 0.1
viscosity = 0.005
axial_unit = 2.0 * math.pi / 20.0
F32 = jnp.float32
BF16 = jnp.bfloat16


def radial_table(count):
    points = np.arange(count)[:, None]
    orders = np.arange(count)[None, :]
    phases = orders * (2 * points + 1) % (4 * count)
    scales = np.where(orders == 0, math.sqrt(1.0 / count), math.sqrt(2.0 / count))
    return np.cos(phases * (math.pi / (2.0 * count))) * scales


def hartley_table(rows, cols, length):
    angles = (rows[:, None] * cols[None, :] % length) * (2.0 * math.pi / length)
    return (np.cos(angles) + np.sin(angles)) / math.sqrt(length)


def halves(table):
    table = np.asarray(table, np.float32)
    high = table.astype(BF16)
    low = (table - high.astype(np.float32)).astype(BF16)
    return np.stack((high, low))


def split(x):
    high = x.astype(BF16)
    return high, (x - high.astype(F32)).astype(BF16)


def table_dot(table, x):
    high, low = split(x)
    left = jnp.concatenate((table[0], table[0], table[1]), axis=1)
    right = jnp.concatenate((high, low, high), axis=0)
    return jnp.dot(left, right, preferred_element_type=F32)


def dot_table(x, table, turned):
    high, low = split(x)
    left = jnp.concatenate((high, low, high), axis=1)
    right = jnp.concatenate((table[0], table[0], table[1]), axis=1 if turned else 0)
    return lax.dot_general(
        left, right, (((1,), (1 if turned else 0,)), ((), ())), preferred_element_type=F32
    )


def spread_kernel(first_ref, second_ref, wide_ref, out_ref, table_ref):
    radial = wide_ref.shape[0]
    rows = radial * 8
    lane = lax.broadcasted_iota(jnp.int32, (8, rows), 1) // radial
    keep = lane == lax.broadcasted_iota(jnp.int32, (8, rows), 0)
    for j in range(radial):
        block = jnp.where(keep, jnp.broadcast_to(wide_ref[j : j + 1, :], (8, rows)), 0.0)
        high, low = split(block)
        table_ref[0, 8 * j : 8 * j + 8, :] = high
        table_ref[1, 8 * j : 8 * j + 8, :] = low
    table = (table_ref[0], table_ref[1])

    def step(index, _):
        c, group = index // 2, index % 2
        start = pl.multiple_of(group * 8, 8)
        x = jnp.concatenate(
            [ref[c, pl.ds(start, 8)].reshape(rows, 128) for ref in (first_ref, second_ref)], axis=1
        )
        y = table_dot(table, x)
        for core in range(2):
            out_ref[:, core, c, pl.ds(start, 8), :] = y[:, 128 * core : 128 * core + 128].reshape(
                radial, 8, 128
            )
        return _

    lax.fori_loop(0, 6, step, 0)


def forward_kernel(recv_ref, azimuth_ref, even_ref, odd_ref, out_ref):
    axial_parts, azimuth_parts, components = recv_ref.shape[:3]
    azimuth_count = azimuth_ref.shape[1]
    half = even_ref.shape[1]
    azimuth = (azimuth_ref[0], azimuth_ref[1])
    even = (even_ref[0], even_ref[1])
    odd = (odd_ref[0], odd_ref[1])

    def step(c, _):
        x = jnp.concatenate(
            [recv_ref[a, :, c].reshape(azimuth_count, 128) for a in range(axial_parts)], axis=1
        )
        y = table_dot(azimuth, x)
        out_ref[c, :, :half] = dot_table(y[:, :half] + y[:, half:], even, False)
        out_ref[c, :, half:] = dot_table(y[:, :half] - y[:, half:], odd, False)
        return _

    lax.fori_loop(0, components, step, 0)


def inverse(rhs, azimuth, even, odd):
    half = even[0].shape[0]
    z = table_dot(azimuth, rhs)
    e = dot_table(z[:, :half], even, False)
    o = dot_table(z[:, half:], odd, True)
    return e + o, e - o


def put(out_ref, c, sides, start):
    for side, y in enumerate(sides):
        for a in range(4):
            block = y[start : start + 128, 128 * a : 128 * a + 128]
            out_ref[4 * side + a, :, c] = block.reshape(16, 8, 128)


def total(ref):
    return ref[0] + ref[1] + ref[2]


def parts(ref):
    return ref[0], ref[1]


def first_product_kernel(own_ref, other_ref, azimuth_ref, even_ref, odd_ref, send_ref, sums_ref):
    core = lax.axis_index("az") % 2
    azimuth = parts(azimuth_ref.at[core])
    sums_ref[0] = total(own_ref)
    sums_ref[1] = total(other_ref)

    def step(c, _):
        rhs = own_ref[c] * sums_ref[1] + other_ref[c] * sums_ref[0]
        put(send_ref, c, inverse(rhs, azimuth, parts(even_ref), parts(odd_ref)), 0)
        return _

    lax.fori_loop(0, 3, step, 0)


def second_kernel(
    recv_ref,
    own_ref,
    azimuth_ref,
    back_ref,
    even_ref,
    odd_ref,
    keep_ref,
    pass_ref,
    field_ref,
    sums_ref,
):
    forward_kernel(recv_ref, azimuth_ref, even_ref, odd_ref, field_ref)
    core = lax.axis_index("az") % 2
    sums_ref[0] = total(own_ref)
    sums_ref[1] = total(field_ref)

    def step(c, _):
        rhs = own_ref[c] * sums_ref[1] + field_ref[c] * sums_ref[0]
        azimuth = tuple(
            jnp.concatenate((back_ref[core, i], back_ref[1 - core, i]), axis=0) for i in range(2)
        )
        sides = inverse(rhs, azimuth, parts(even_ref), parts(odd_ref))
        put(keep_ref, c, sides, 0)
        put(pass_ref, c, sides, 128)
        return _

    lax.fori_loop(0, 3, step, 0)


def gather_kernel(recv_ref, field_ref, rate_ref, tall_ref, out_ref, table_ref):
    radial = tall_ref.shape[0]
    rows = radial * 8
    lane = lax.broadcasted_iota(jnp.int32, (radial, rows), 1) % 8
    for m in range(8):
        high, low = split(jnp.where(lane == m, tall_ref[...], 0.0))
        table_ref[0, radial * m : radial * m + radial, :] = high
        table_ref[1, radial * m : radial * m + radial, :] = low
    table = (table_ref[0], table_ref[1])
    azimuth_count, axial_count = 256, 1024
    axial = lax.axis_index("ax") * 128 + lax.broadcasted_iota(jnp.int32, (1, 128), 1)
    wave = jnp.minimum(axial, axial_count - axial).astype(F32) * axial_unit
    base = rate_ref[...] + wave * wave

    def step(c, _):
        x = jnp.concatenate([recv_ref[:, core, c].reshape(rows, 128) for core in range(2)], axis=1)
        y = table_dot(table, x)
        for core in range(2):
            for i in range(8):
                m = 8 * core + i
                azimuth = lax.axis_index("az") * 16 + m
                wave_azimuth = jnp.minimum(azimuth, azimuth_count - azimuth).astype(F32)
                denom = 1.0 + viscosity * (base + wave_azimuth * wave_azimuth)
                term = y[radial * i : radial * i + radial, 128 * core : 128 * core + 128]
                out_ref[c, m] = (field_ref[c, m] + time_step * term) / denom
        return _

    lax.fori_loop(0, 3, step, 0)


def call(kernel, shape, *args, scratch=(), limit=16):
    many = isinstance(shape, list)
    vmem = pl.BlockSpec(memory_space=pltpu.VMEM)
    return pl.pallas_call(
        kernel,
        out_shape=[jax.ShapeDtypeStruct(x, F32) for x in shape] if many else jax.ShapeDtypeStruct(shape, F32),
        in_specs=[vmem] * len(args),
        out_specs=[vmem] * len(shape) if many else vmem,
        scratch_shapes=list(scratch),
        compiler_params=pltpu.CompilerParams(vmem_limit_bytes=limit * 1024 * 1024),
    )(*args)


def body(saved_flow, saved_adjoint, tangent, second_adjoint, radial_rate):
    radial = radial_table(64)
    wide = np.tile(radial, (1, 8)).astype(np.float32)
    tall = np.repeat(radial.T, 8, axis=1).astype(np.float32)
    order = np.arange(256)
    azimuth = halves(hartley_table(order, order, 256))
    kept = [[16 * a + 8 * s + i for a in range(16) for i in range(8)] for s in range(2)]
    azimuth_back = np.stack([halves(hartley_table(np.array(rows), order, 256)) for rows in kept])
    line = np.arange(512)
    even = halves(hartley_table(line, 2 * line, 1024))
    odd = halves(hartley_table(line, 2 * line + 1, 1024))
    rate = jnp.broadcast_to(radial_rate[:, None], (64, 128))
    pairs = [(i, i ^ 1) for i in range(16)]
    table_scratch = (pltpu.VMEM((2, 512, 512), BF16),)

    def grid(count):
        return (pltpu.VMEM((count, 256, 1024), F32),)

    def spread(first, second):
        return call(spread_kernel, (64, 2, 3, 16, 128), first, second, wide, scratch=table_scratch)

    def whole(x):
        x = x.reshape((128,) + x.shape[2:])
        return lax.all_to_all(x, ("ax", "az"), 0, 0, tiled=True)

    def planes(x):
        return x.reshape(8, 16, 3, 16, 128)

    def gather(x, field):
        return call(
            gather_kernel,
            (3, 16, 64, 128),
            x.reshape(64, 2, 3, 8, 128),
            field,
            rate,
            tall,
            scratch=table_scratch,
        )

    back = (8, 16, 3, 8, 128)
    first = whole(spread(saved_flow, tangent))
    second = whole(spread(second_adjoint, saved_adjoint))
    own = call(forward_kernel, (3, 256, 1024), planes(first), azimuth, even, odd, limit=24)
    other = lax.ppermute(own, "az", pairs)
    tangent_send = call(
        first_product_kernel, back, own, other, azimuth_back, even, odd, scratch=grid(2), limit=24
    )
    tangent_back = whole(tangent_send)
    keep, passed = call(
        second_kernel,
        [back, back],
        planes(second),
        own,
        azimuth,
        azimuth_back,
        even,
        odd,
        scratch=grid(3) + grid(2),
        limit=32,
    )
    second_send = keep + lax.ppermute(passed, "az", pairs)
    tangent_next = gather(tangent_back, tangent)
    second_next = gather(whole(second_send), second_adjoint)
    return (tangent_next, second_next)


def solution(mesh):
    spec = P(None, "az", None, "ax")
    return jax.shard_map(
        body, mesh=mesh, in_specs=(spec,) * 4 + (P(),), out_specs=(spec, spec), check_vma=False
    )
```

```python
import math

import jax
import jax.numpy as jnp
import numpy as np
from jax import lax
from jax.experimental import pallas as pl
from jax.experimental.pallas import tpu as pltpu
from jax.sharding import PartitionSpec as P

time_step = 0.1
viscosity = 0.005
axial_unit = 2.0 * math.pi / 20.0
F32 = jnp.float32
BF16 = jnp.bfloat16


def radial_table(count):
    points = np.arange(count)[:, None]
    orders = np.arange(count)[None, :]
    phases = orders * (2 * points + 1) % (4 * count)
    scales = np.where(orders == 0, math.sqrt(1.0 / count), math.sqrt(2.0 / count))
    return np.cos(phases * (math.pi / (2.0 * count))) * scales


def hartley_table(rows, cols, length):
    angles = (rows[:, None] * cols[None, :] % length) * (2.0 * math.pi / length)
    return (np.cos(angles) + np.sin(angles)) / math.sqrt(length)


def halves(table):
    table = np.asarray(table, np.float32)
    high = table.astype(BF16)
    low = (table - high.astype(np.float32)).astype(BF16)
    return np.stack((high, low))


def split(x):
    high = x.astype(BF16)
    return high, (x - high.astype(F32)).astype(BF16)


def table_dot(table, x):
    high, low = split(x)
    left = jnp.concatenate((table[0], table[0], table[1]), axis=1)
    right = jnp.concatenate((high, low, high), axis=0)
    return jnp.dot(left, right, preferred_element_type=F32)


def dot_table(x, table, turned):
    high, low = split(x)
    left = jnp.concatenate((high, low, high), axis=1)
    right = jnp.concatenate((table[0], table[0], table[1]), axis=1 if turned else 0)
    return lax.dot_general(
        left, right, (((1,), (1 if turned else 0,)), ((), ())), preferred_element_type=F32
    )


def parts(ref):
    return ref[0], ref[1]


def low_half(shape):
    return lax.broadcasted_iota(jnp.int32, shape, len(shape) - 2) % 8 < 4


def spread_kernel(flow_ref, tangent_ref, second_ref, adjoint_ref, wide_ref, out_ref, table_ref):
    fields = (flow_ref, second_ref, tangent_ref, adjoint_ref)
    radial, rows = wide_ref.shape
    low = low_half((8, rows))

    @pl.when(pl.program_id(0) == 0)
    def _():
        lane = lax.broadcasted_iota(jnp.int32, (8, rows), 1) // radial
        keep = lane == lax.broadcasted_iota(jnp.int32, (8, rows), 0) % 4
        for p in range(radial // 2):
            one = jnp.broadcast_to(wide_ref[2 * p : 2 * p + 1, :], (8, rows))
            two = jnp.broadcast_to(wide_ref[2 * p + 1 : 2 * p + 2, :], (8, rows))
            for half, (first, last) in enumerate(((one, two), (two, one))):
                pair = split(jnp.where(keep, jnp.where(low, first, last), 0.0))
                for i in range(2):
                    table_ref[half, i, 8 * p : 8 * p + 8, :] = pair[i]

    def step(group, _):
        start = pl.multiple_of(group * 8, 8)
        y = []
        for half in range(2):
            x = jnp.concatenate(
                [ref[0, pl.ds(start + 4 * half, 4)].reshape(rows, 128) for ref in fields], axis=1
            )
            y.append(table_dot(parts(table_ref.at[half]), x).reshape(radial // 2, 8, 512))
        first = low_half(y[0].shape)
        even = jnp.where(first, y[0], y[1])
        odd = pltpu.roll(jnp.where(first, y[1], y[0]), 4, 1)
        for parity, z in enumerate((even, odd)):
            for core in range(2):
                for which in range(2):
                    lane = 128 * (2 * core + which)
                    out_ref[:, parity, core, which, 0, pl.ds(start, 8), :] = z[:, :, lane : lane + 128]
        return _

    lax.fori_loop(0, 2, step, 0)


def forward(x, azimuth, axial):
    y = table_dot(azimuth, x)
    s = y[:, :512] + y[:, 512:]
    d = y[:, :512] - y[:, 512:]
    return jnp.concatenate(
        (
            dot_table(s[:, :256] + s[:, 256:], axial[0], False),
            dot_table(s[:, :256] - s[:, 256:], axial[1], False),
            dot_table(d, axial[2], False),
        ),
        axis=1,
    )


def backward(z, axial):
    a = dot_table(z[:, :256], axial[0], True)
    b = dot_table(z[:, 256:512], axial[1], True)
    o = dot_table(z[:, 512:], axial[2], True)
    e = jnp.concatenate((a + b, a - b), axis=1)
    return e + o, e - o


def plane(recv_ref, c):
    return jnp.concatenate([recv_ref[a, :, c].reshape(256, 128) for a in range(8)], axis=1)


def first_kernel(recv_ref, azimuth_ref, zero_ref, two_ref, odd_ref, out_ref):
    def step(c, _):
        axial = (parts(zero_ref), parts(two_ref), parts(odd_ref))
        out_ref[c] = forward(plane(recv_ref, c), parts(azimuth_ref), axial)
        return _

    lax.fori_loop(0, 3, step, 0)


def total(ref):
    return ref[0] + ref[1] + ref[2]


def second_kernel(
    recv_ref,
    own_ref,
    azimuth_ref,
    back_ref,
    zero_ref,
    two_ref,
    odd_ref,
    keep_ref,
    pass_ref,
    field_ref,
    sums_ref,
):
    def step(c, _):
        axial = (parts(zero_ref), parts(two_ref), parts(odd_ref))
        field_ref[c] = forward(plane(recv_ref, 3 + c), parts(azimuth_ref), axial)
        return _

    lax.fori_loop(0, 3, step, 0)
    core = lax.axis_index("az") % 2
    sums_ref[0] = total(own_ref)
    sums_ref[1] = total(field_ref)

    def product(c, _):
        rhs = own_ref[c] * sums_ref[1] + field_ref[c] * sums_ref[0]
        azimuth = tuple(
            jnp.concatenate((back_ref[core, i], back_ref[1 - core, i]), axis=0) for i in range(2)
        )
        z = table_dot(azimuth, rhs)
        keep_ref[c] = z[:128]
        pass_ref[c] = z[128:]
        return _

    lax.fori_loop(0, 3, product, 0)


def tangent_kernel(own_ref, other_ref, back_ref, out_ref, sums_ref):
    core = lax.axis_index("az") % 2
    sums_ref[0] = total(own_ref)
    sums_ref[1] = total(other_ref)

    def step(c, _):
        rhs = own_ref[c] * sums_ref[1] + other_ref[c] * sums_ref[0]
        out_ref[c] = table_dot(parts(back_ref.at[core]), rhs)
        return _

    lax.fori_loop(0, 3, step, 0)


def backward_kernel(tangent_ref, keep_ref, other_ref, zero_ref, two_ref, odd_ref, send_ref):
    axial = (parts(zero_ref), parts(two_ref), parts(odd_ref))
    for group in range(2):
        z = tangent_ref[...] if group == 0 else keep_ref[...] + other_ref[...]
        for side, y in enumerate(backward(z.reshape(384, 1024), axial)):
            for a in range(4):
                for c in range(3):
                    block = y[128 * c : 128 * c + 128, 128 * a : 128 * a + 128]
                    send_ref[4 * side + a, :, 3 * group + c] = block.reshape(16, 8, 128)


def gather_kernel(
    recv_ref, tangent_ref, second_ref, rate_ref, tall_ref, out_ref, out2_ref, table_ref, scale_ref
):
    radial, rows = tall_ref.shape[1:]
    azimuth_count, axial_count = 256, 1024

    @pl.when(pl.program_id(0) == 0)
    def _():
        lane = lax.broadcasted_iota(jnp.int32, (radial, rows), 1) % 4
        for half in range(2):
            for m in range(4):
                pair = split(jnp.where(lane == m, tall_ref[half], 0.0))
                for i in range(2):
                    table_ref[half, i, radial * m : radial * m + radial, :] = pair[i]
        axial = lax.axis_index("ax") * 128 + lax.broadcasted_iota(jnp.int32, (1, 128), 1)
        wave = jnp.minimum(axial, axial_count - axial).astype(F32) * axial_unit
        base = rate_ref[...] + wave * wave
        for m in range(16):
            azimuth = lax.axis_index("az") * 16 + m
            wave_azimuth = jnp.minimum(azimuth, azimuth_count - azimuth).astype(F32)
            scale_ref[m] = 1.0 / (1.0 + viscosity * (base + wave_azimuth * wave_azimuth))

    x = jnp.concatenate(
        [
            recv_ref[:, :, core, which, 0].reshape(32, 2, 8, 128)
            for core in range(2)
            for which in range(2)
        ],
        axis=3,
    )
    even, odd = x[:, 0], pltpu.roll(x[:, 1], 4, 1)
    first = low_half(even.shape)
    for half in range(2):
        z = jnp.where(first, even, odd) if half == 0 else jnp.where(first, odd, even)
        y = table_dot(parts(table_ref.at[half]), z.reshape(rows, 512))
        for core in range(2):
            for which, (field, out) in enumerate(((tangent_ref, out_ref), (second_ref, out2_ref))):
                lane = 128 * (2 * core + which)
                for i in range(4):
                    m = 8 * core + 4 * half + i
                    term = y[radial * i : radial * i + radial, lane : lane + 128]
                    out[0, m] = (field[0, m] + time_step * term) * scale_ref[m]


WHOLE = pl.BlockSpec(memory_space=pltpu.VMEM)


def call(kernel, shapes, *args, scratch=(), limit=24, specs=None, out_specs=None, grid=()):
    out = [jax.ShapeDtypeStruct(shape, F32) for shape in shapes]
    return pl.pallas_call(
        kernel,
        out_shape=out,
        grid=grid,
        in_specs=specs or [WHOLE] * len(args),
        out_specs=out_specs or [WHOLE] * len(out),
        scratch_shapes=list(scratch),
        compiler_params=pltpu.CompilerParams(vmem_limit_bytes=limit * 1024 * 1024),
    )(*args)


def by_component(shape, axis):
    block = shape[:axis] + (1,) + shape[axis + 1 :]
    return pl.BlockSpec(block, lambda c: tuple(c if i == axis else 0 for i in range(len(shape))))


def body(saved_flow, saved_adjoint, tangent, second_adjoint, radial_rate):
    radial = radial_table(64)
    wide = np.tile(radial, (1, 4)).astype(np.float32)
    column = np.arange(256)
    swapped = 2 * (column // 8) + 1 - column % 8 // 4
    tall = np.stack((radial.T[:, column // 4], radial.T[:, swapped])).astype(np.float32)
    order = np.arange(256)
    azimuth = halves(hartley_table(order, order, 256))
    kept = [[16 * a + 8 * s + i for a in range(16) for i in range(8)] for s in range(2)]
    back = np.stack([halves(hartley_table(np.array(rows), order, 256)) for rows in kept])
    axial = (
        halves(hartley_table(order, 4 * order, 1024)),
        halves(hartley_table(order, 4 * order + 2, 1024)),
        halves(hartley_table(np.arange(512), 2 * np.arange(512) + 1, 1024)),
    )
    rate = jnp.broadcast_to(radial_rate[:, None], (64, 128))
    pairs = [(i, i ^ 1) for i in range(16)]
    field = by_component((3, 16, 64, 128), 0)

    def swap(x):
        return lax.ppermute(x, "az", pairs)

    def whole(x):
        return lax.all_to_all(x, ("ax", "az"), 0, 0, tiled=True)

    sent = (32, 2, 2, 2, 3, 16, 128)
    (spread,) = call(
        spread_kernel,
        [sent],
        saved_flow,
        tangent,
        second_adjoint,
        saved_adjoint,
        wide,
        scratch=(pltpu.VMEM((2, 2, 256, 256), BF16),),
        specs=[field] * 4 + [pl.BlockSpec((64, 256), lambda c: (0, 0))],
        out_specs=[by_component(sent, 4)],
        grid=(3,),
    )
    recv = whole(spread.reshape(128, 6, 16, 128)).reshape(8, 16, 6, 16, 128)
    (own,) = call(first_kernel, [(3, 256, 1024)], recv, azimuth, *axial)
    other = swap(own)
    keep, passed = call(
        second_kernel,
        [(3, 128, 1024)] * 2,
        recv,
        own,
        azimuth,
        back,
        *axial,
        scratch=(pltpu.VMEM((3, 256, 1024), F32), pltpu.VMEM((2, 256, 1024), F32)),
    )
    joined = swap(passed)
    (turned,) = call(
        tangent_kernel,
        [(3, 128, 1024)],
        own,
        other,
        back,
        scratch=(pltpu.VMEM((2, 256, 1024), F32),),
    )
    (send,) = call(backward_kernel, [(8, 16, 6, 8, 128)], turned, keep, joined, *axial)
    final = (32, 2, 2, 2, 3, 8, 128)
    back_home = whole(send.reshape(128, 6, 8, 128)).reshape(final)
    shape = tangent.shape
    return tuple(
        call(
            gather_kernel,
            [shape, shape],
            back_home,
            tangent,
            second_adjoint,
            rate,
            tall,
            scratch=(pltpu.VMEM((2, 2, 256, 256), BF16), pltpu.VMEM((16, 64, 128), F32)),
            specs=[by_component(final, 4), field, field]
            + [pl.BlockSpec((64, 128), lambda c: (0, 0)), pl.BlockSpec((2, 64, 256), lambda c: (0, 0, 0))],
            out_specs=[field, field],
            grid=(3,),
        )
    )


def solution(mesh):
    spec = P(None, "az", None, "ax")
    return jax.shard_map(
        body, mesh=mesh, in_specs=(spec,) * 4 + (P(),), out_specs=(spec, spec), check_vma=False
    )
```

```python
import math

import jax
import jax.numpy as jnp
import numpy as np
from jax import lax
from jax.experimental import pallas as pl
from jax.experimental.pallas import tpu as pltpu
from jax.sharding import PartitionSpec as P

time_step = 0.1
viscosity = 0.005
axial_unit = 2.0 * math.pi / 20.0
F32 = jnp.float32
BF16 = jnp.bfloat16


def radial_table(count):
    points = np.arange(count)[:, None]
    orders = np.arange(count)[None, :]
    phases = orders * (2 * points + 1) % (4 * count)
    scales = np.where(orders == 0, math.sqrt(1.0 / count), math.sqrt(2.0 / count))
    return np.cos(phases * (math.pi / (2.0 * count))) * scales


def hartley_table(rows, cols, length):
    angles = (rows[:, None] * cols[None, :] % length) * (2.0 * math.pi / length)
    return (np.cos(angles) + np.sin(angles)) / math.sqrt(length)


def halves(table):
    table = np.asarray(table, np.float32)
    high = table.astype(BF16)
    low = (table - high.astype(np.float32)).astype(BF16)
    return np.stack((high, low))


def split(x):
    high = x.astype(BF16)
    return high, (x - high.astype(F32)).astype(BF16)


def table_dot(table, x):
    high, low = split(x)
    left = jnp.concatenate((table[0], table[0], table[1]), axis=1)
    right = jnp.concatenate((high, low, high), axis=0)
    return jnp.dot(left, right, preferred_element_type=F32)


def dot_table(x, table, turned):
    high, low = split(x)
    left = jnp.concatenate((high, low, high), axis=1)
    right = jnp.concatenate((table[0], table[0], table[1]), axis=1 if turned else 0)
    return lax.dot_general(
        left, right, (((1,), (1 if turned else 0,)), ((), ())), preferred_element_type=F32
    )


def parts(ref):
    return ref[0], ref[1]


def low_half(shape):
    return lax.broadcasted_iota(jnp.int32, shape, len(shape) - 2) % 8 < 4


def spread_kernel(
    flow_ref, tangent_ref, second_ref, adjoint_ref, wide_ref, out_ref, table_ref, field_ref, sems
):
    radial, rows = wide_ref.shape

    def fetch(i, ref, step):
        c, start = step // 2, pl.multiple_of(step % 2 * 8, 8)
        place = (c, pl.ds(start, 8))
        return pltpu.make_async_copy(ref.at[place], field_ref.at[(i, *place)], sems.at[i, step])

    fields = tuple(enumerate((flow_ref, second_ref, tangent_ref, adjoint_ref)))
    for step in range(6):
        for i, ref in fields:
            fetch(i, ref, step).start()
    low = low_half((8, rows))
    lane = lax.broadcasted_iota(jnp.int32, (8, rows), 1) // radial
    keep = lane == lax.broadcasted_iota(jnp.int32, (8, rows), 0) % 4
    for p in range(radial // 2):
        one = jnp.broadcast_to(wide_ref[2 * p : 2 * p + 1, :], (8, rows))
        two = jnp.broadcast_to(wide_ref[2 * p + 1 : 2 * p + 2, :], (8, rows))
        for half, (first, last) in enumerate(((one, two), (two, one))):
            pair = split(jnp.where(keep, jnp.where(low, first, last), 0.0))
            for i in range(2):
                table_ref[half, i, 8 * p : 8 * p + 8, :] = pair[i]

    def work(step, _):
        for i, ref in fields:
            fetch(i, ref, step).wait()
        c, start = step // 2, pl.multiple_of(step % 2 * 8, 8)
        y = []
        for half in range(2):
            x = jnp.concatenate(
                [field_ref[i, c, pl.ds(start + 4 * half, 4)].reshape(rows, 128) for i in range(4)],
                axis=1,
            )
            y.append(table_dot(parts(table_ref.at[half]), x).reshape(radial // 2, 8, 512))
        first = low_half(y[0].shape)
        even = jnp.where(first, y[0], y[1])
        odd = pltpu.roll(jnp.where(first, y[1], y[0]), 4, 1)
        for parity, z in enumerate((even, odd)):
            for core in range(2):
                for which in range(2):
                    lane = 128 * (2 * core + which)
                    out_ref[:, parity, core, which, c, pl.ds(start, 8), :] = z[:, :, lane : lane + 128]
        return _

    lax.fori_loop(0, 6, work, 0)


def forward(x, azimuth, axial):
    y = jnp.concatenate(
        (table_dot(azimuth[0], x[:128] + x[128:]), table_dot(azimuth[1], x[:128] - x[128:])), axis=0
    )
    s = y[:, :512] + y[:, 512:]
    d = y[:, :512] - y[:, 512:]
    return jnp.concatenate(
        (
            dot_table(s[:, :256] + s[:, 256:], axial[0], False),
            dot_table(s[:, :256] - s[:, 256:], axial[1], False),
            dot_table(d, axial[2], False),
        ),
        axis=1,
    )


def backward(z, axial):
    a = dot_table(z[:, :256], axial[0], True)
    b = dot_table(z[:, 256:512], axial[1], True)
    o = dot_table(z[:, 512:], axial[2], True)
    e = jnp.concatenate((a + b, a - b), axis=1)
    return e + o, e - o


def plane(recv_ref, c):
    return jnp.concatenate([recv_ref[a, :, c].reshape(256, 128) for a in range(8)], axis=1)


def put(z, axial, send_ref, group):
    for side, y in enumerate(backward(z, axial)):
        for a in range(4):
            for c in range(3):
                block = y[128 * c : 128 * c + 128, 128 * a : 128 * a + 128]
                send_ref[4 * side + a, :, 3 * group + c] = block.reshape(16, 8, 128)


def add_to(sum_ref, c, value):
    sum_ref[...] = jnp.where(c == 0, 0.0, sum_ref[...]) + value


def first_kernel(recv_ref, azimuth_ref, zero_ref, two_ref, odd_ref, out_ref, sum_ref):
    def step(c, _):
        axial = (parts(zero_ref), parts(two_ref), parts(odd_ref))
        azimuth = (parts(azimuth_ref.at[0]), parts(azimuth_ref.at[1]))
        y = forward(plane(recv_ref, c), azimuth, axial)
        out_ref[c] = y
        add_to(sum_ref, c, y)
        return _

    lax.fori_loop(0, 3, step, 0)


def second_kernel(
    recv_ref,
    own_ref,
    own_sum_ref,
    azimuth_ref,
    back_ref,
    zero_ref,
    two_ref,
    odd_ref,
    keep_ref,
    pass_ref,
    field_ref,
    sum_ref,
):
    def step(c, _):
        axial = (parts(zero_ref), parts(two_ref), parts(odd_ref))
        azimuth = (parts(azimuth_ref.at[0]), parts(azimuth_ref.at[1]))
        y = forward(plane(recv_ref, 3 + c), azimuth, axial)
        field_ref[c] = y
        add_to(sum_ref, c, y)
        return _

    lax.fori_loop(0, 3, step, 0)
    core = lax.axis_index("az") % 2

    def product(c, _):
        rhs = own_ref[c] * sum_ref[...] + field_ref[c] * own_sum_ref[...]
        side = []
        for parity in range(2):
            table = tuple(
                jnp.concatenate((back_ref[core, parity, i], back_ref[1 - core, parity, i]), axis=0)
                for i in range(2)
            )
            side.append(table_dot(table, rhs[128 * parity : 128 * parity + 128]))
        upper, lower = side[0] + side[1], side[0] - side[1]
        keep_ref[c] = jnp.concatenate((upper[:64], lower[:64]), axis=0)
        pass_ref[c] = jnp.concatenate((upper[64:], lower[64:]), axis=0)
        return _

    lax.fori_loop(0, 3, product, 0)


def tangent_kernel(
    own_ref,
    own_sum_ref,
    other_ref,
    back_ref,
    zero_ref,
    two_ref,
    odd_ref,
    send_ref,
    sum_ref,
    turned_ref,
):
    core = lax.axis_index("az") % 2
    sum_ref[...] = other_ref[0] + other_ref[1] + other_ref[2]

    def step(c, _):
        rhs = own_ref[c] * sum_ref[...] + other_ref[c] * own_sum_ref[...]
        e = table_dot(parts(back_ref.at[core, 0]), rhs[:128])
        o = table_dot(parts(back_ref.at[core, 1]), rhs[128:])
        turned_ref[c] = jnp.concatenate((e + o, e - o), axis=0)
        return _

    lax.fori_loop(0, 3, step, 0)
    axial = (parts(zero_ref), parts(two_ref), parts(odd_ref))
    put(turned_ref[...].reshape(384, 1024), axial, send_ref, 0)


def join_kernel(tangent_ref, keep_ref, other_ref, zero_ref, two_ref, odd_ref, send_ref):
    send_ref[:, :, :3] = tangent_ref[...]
    z = keep_ref[...] + other_ref[...]
    put(z.reshape(384, 1024), (parts(zero_ref), parts(two_ref), parts(odd_ref)), send_ref, 1)


def gather_kernel(
    recv_ref, tangent_ref, second_ref, rate_ref, table_ref, out_ref, out2_ref, result_ref, scale_ref, sems
):
    radial = rate_ref.shape[0]
    azimuth_count, axial_count = 256, 1024
    axial = lax.axis_index("ax") * 128 + lax.broadcasted_iota(jnp.int32, (1, 128), 1)
    wave = jnp.minimum(axial, axial_count - axial).astype(F32) * axial_unit
    base = rate_ref[...] + wave * wave

    def scale(m, _):
        azimuth = lax.axis_index("az") * 16 + m
        wave_azimuth = jnp.minimum(azimuth, azimuth_count - azimuth).astype(F32)
        scale_ref[m] = 1.0 / (1.0 + viscosity * (base + wave_azimuth * wave_azimuth))
        return _

    lax.fori_loop(0, 16, scale, 0)
    outs = (out_ref, out2_ref)
    fields = (tangent_ref, second_ref)

    def give(which, c, core):
        place = (c, pl.ds(8 * core, 8))
        return pltpu.make_async_copy(
            result_ref.at[(which, *place)], outs[which].at[place], sems.at[which, c, core]
        )

    def step(c, _):
        x = jnp.concatenate(
            [recv_ref[:, :, core, which, c] for core in range(2) for which in range(2)], axis=3
        )
        even, odd = x[:, 0], pltpu.roll(x[:, 1], 4, 1)
        first = low_half(even.shape)
        for half in range(2):
            z = jnp.where(first, even, odd) if half == 0 else jnp.where(first, odd, even)
            y = table_dot(parts(table_ref.at[half]), z.reshape(4 * radial, 512))
            for core in range(2):
                for which in range(2):
                    lane = 128 * (2 * core + which)
                    for i in range(4):
                        m = 8 * core + 4 * half + i
                        term = y[radial * i : radial * i + radial, lane : lane + 128]
                        result_ref[which, c, m] = (fields[which][c, m] + time_step * term) * scale_ref[m]
        for which in range(2):
            for core in range(2):
                give(which, c, core).start()
        return _

    lax.fori_loop(0, 3, step, 0)

    def finish(c, _):
        for which in range(2):
            for core in range(2):
                give(which, c, core).wait()
        return _

    lax.fori_loop(0, 3, finish, 0)


WHOLE = pl.BlockSpec(memory_space=pltpu.VMEM)
LEFT = pl.BlockSpec(memory_space=pl.ANY)


def call(kernel, shapes, *args, scratch=(), limit=24, specs=None, out_spec=WHOLE):
    out = [jax.ShapeDtypeStruct(shape, F32) for shape in shapes]
    return pl.pallas_call(
        kernel,
        out_shape=out,
        in_specs=specs or [WHOLE] * len(args),
        out_specs=[out_spec] * len(out),
        scratch_shapes=list(scratch),
        compiler_params=pltpu.CompilerParams(vmem_limit_bytes=limit * 1024 * 1024),
    )(*args)


def gather_table(radial):
    column = np.arange(256)
    swapped = 2 * (column // 8) + 1 - column % 8 // 4
    sides = []
    for j in (column // 4, swapped):
        keep = np.arange(4)[:, None, None] == (column % 4)[None, None, :]
        sides.append(halves(np.where(keep, radial.T[:, j][None], 0.0).reshape(256, 256)))
    return np.stack(sides)


def body(saved_flow, saved_adjoint, tangent, second_adjoint, radial_rate):
    radial = radial_table(64)
    wide = np.tile(radial, (1, 4)).astype(np.float32)
    half, quarter = np.arange(128), np.arange(256)
    azimuth = np.stack([halves(hartley_table(2 * half + p, half, 256)) for p in range(2)])
    kept = [np.array([16 * a + 8 * s + i for a in range(8) for i in range(8)]) for s in range(2)]
    back = np.stack(
        [
            np.stack([halves(hartley_table(rows, 2 * half + p, 256)) for p in range(2)])
            for rows in kept
        ]
    )
    axial = (
        halves(hartley_table(quarter, 4 * quarter, 1024)),
        halves(hartley_table(quarter, 4 * quarter + 2, 1024)),
        halves(hartley_table(np.arange(512), 2 * np.arange(512) + 1, 1024)),
    )
    rate = jnp.broadcast_to(radial_rate[:, None], (64, 128))
    pairs = [(i, i ^ 1) for i in range(16)]
    grid, rows = (256, 1024), (128, 1024)

    def swap(x):
        return lax.ppermute(x, "az", pairs)

    def whole(x):
        return lax.all_to_all(x, ("ax", "az"), 0, 0, tiled=True)

    (spread,) = call(
        spread_kernel,
        [(32, 2, 2, 2, 3, 16, 128)],
        *(
            pltpu.with_memory_space_constraint(x, pltpu.HBM)
            for x in (saved_flow, tangent, second_adjoint, saved_adjoint)
        ),
        wide,
        scratch=(
            pltpu.VMEM((2, 2, 256, 256), BF16),
            pltpu.VMEM((4, 3, 16, 64, 128), F32),
            pltpu.SemaphoreType.DMA((4, 6)),
        ),
        specs=[LEFT] * 4 + [WHOLE],
    )
    recv = whole(spread.reshape(128, 6, 16, 128)).reshape(8, 16, 6, 16, 128)
    own, own_sum = call(first_kernel, [(3, *grid), grid], recv, azimuth, *axial)
    other = swap(own)
    keep, passed = call(
        second_kernel,
        [(3, *rows)] * 2,
        recv,
        own,
        own_sum,
        azimuth,
        back,
        *axial,
        scratch=(pltpu.VMEM((3, *grid), F32), pltpu.VMEM(grid, F32)),
    )
    joined = swap(passed)
    (turned,) = call(
        tangent_kernel,
        [(8, 16, 3, 8, 128)],
        own,
        own_sum,
        other,
        back,
        *axial,
        scratch=(pltpu.VMEM(grid, F32), pltpu.VMEM((3, *rows), F32)),
    )
    (send,) = call(join_kernel, [(8, 16, 6, 8, 128)], turned, keep, joined, *axial)
    home = whole(send.reshape(128, 6, 8, 128)).reshape(32, 2, 2, 2, 3, 8, 128)
    shape = tangent.shape
    return tuple(
        call(
            gather_kernel,
            [shape, shape],
            home,
            tangent,
            second_adjoint,
            rate,
            gather_table(radial),
            scratch=(
                pltpu.VMEM((2, *shape), F32),
                pltpu.VMEM(shape[1:], F32),
                pltpu.SemaphoreType.DMA((2, 3, 2)),
            ),
            out_spec=LEFT,
        )
    )


def solution(mesh):
    spec = P(None, "az", None, "ax")
    return jax.shard_map(
        body, mesh=mesh, in_specs=(spec,) * 4 + (P(),), out_specs=(spec, spec), check_vma=False
    )
```

```python
import math

import jax
import jax.numpy as jnp
import numpy as np
from jax import lax
from jax.experimental import pallas as pl
from jax.experimental.pallas import tpu as pltpu
from jax.sharding import PartitionSpec as P

time_step = 0.1
viscosity = 0.005
axial_unit = 2.0 * math.pi / 20.0
F32 = jnp.float32
BF16 = jnp.bfloat16


def radial_table(count):
    points = np.arange(count)[:, None]
    orders = np.arange(count)[None, :]
    phases = orders * (2 * points + 1) % (4 * count)
    scales = np.where(orders == 0, math.sqrt(1.0 / count), math.sqrt(2.0 / count))
    return np.cos(phases * (math.pi / (2.0 * count))) * scales


def hartley_table(rows, cols, length):
    angles = (rows[:, None] * cols[None, :] % length) * (2.0 * math.pi / length)
    return (np.cos(angles) + np.sin(angles)) / math.sqrt(length)


def halves(table):
    table = np.asarray(table, np.float32)
    high = table.astype(BF16)
    low = (table - high.astype(np.float32)).astype(BF16)
    return np.stack((high, low))


def split(x):
    high = x.astype(BF16)
    return high, (x - high.astype(F32)).astype(BF16)


def stacked(table):
    high, low = halves(table)
    return np.block([[high, high], [low, np.zeros_like(low)]])


def table_dot(table, x):
    out = jnp.dot(table, jnp.concatenate(split(x), axis=0), preferred_element_type=F32)
    half = out.shape[0] // 2
    return out[:half] + out[half:]


def dot_table(x, table, turned):
    high, low = split(x)
    left = jnp.concatenate((high, low, high), axis=1)
    right = jnp.concatenate((table[0], table[0], table[1]), axis=1 if turned else 0)
    return lax.dot_general(
        left, right, (((1,), (1 if turned else 0,)), ((), ())), preferred_element_type=F32
    )


def parts(ref):
    return ref[0], ref[1]


def pick(arrays, first, step):
    block = lax.broadcasted_iota(jnp.int32, arrays[0].shape, 1) // 2
    out = arrays[first % 4]
    for b in range(1, 4):
        out = jnp.where(block == b, arrays[(first + step * b) % 4], out)
    return out


def spread_kernel(
    flow_ref,
    tangent_ref,
    second_ref,
    adjoint_ref,
    radial_ref,
    out_ref,
    table_ref,
    field_ref,
    sem,
    sems,
):
    fetch_table = pltpu.make_async_copy(radial_ref, table_ref, sem)

    def fetch(i, ref, step):
        c, start = step // 2, pl.multiple_of(step % 2 * 8, 8)
        place = (c, pl.ds(start, 8))
        return pltpu.make_async_copy(ref.at[place], field_ref.at[(i, *place)], sems.at[i, step])

    fields = tuple(enumerate((flow_ref, second_ref, tangent_ref, adjoint_ref)))
    for step in range(6):
        for i, ref in fields:
            fetch(i, ref, step).start(priority=i % 2)
        if step == 0:
            fetch_table.start()
    fetch_table.wait()

    def work(step, _):
        for i, ref in fields:
            fetch(i, ref, step).wait()
        c, start = step // 2, pl.multiple_of(step % 2 * 8, 8)
        y = []
        for p in range(4):
            x = []
            for n in range(2):
                m = start + 2 * p + n
                x.extend(split(jnp.concatenate([field_ref[i, c, m] for i in range(4)], axis=1)))
            out = jnp.dot(
                table_ref[p], jnp.concatenate(x, axis=0), preferred_element_type=F32
            )
            y.append((out[:128] + out[128:]).reshape(16, 8, 512))
        for q in range(4):
            z = pick(y, q, 1)
            z = pltpu.roll(z, 2 * q, 1) if q else z
            for i in range(4):
                out_ref[:, q, i, c, pl.ds(start, 8), :] = z[:, :, 128 * i : 128 * i + 128]
        return _

    lax.fori_loop(0, 6, work, 0)


def forward(x, azimuth, axial):
    y = jnp.concatenate(
        (table_dot(azimuth[0], x[:128] + x[128:]), table_dot(azimuth[1], x[:128] - x[128:])), axis=0
    )
    s = y[:, :512] + y[:, 512:]
    d = y[:, :512] - y[:, 512:]
    return jnp.concatenate(
        (
            dot_table(s[:, :256] + s[:, 256:], axial[0], False),
            dot_table(s[:, :256] - s[:, 256:], axial[1], False),
            dot_table(d, axial[2], False),
        ),
        axis=1,
    )


def backward(z, axial):
    a = dot_table(z[:, :256], axial[0], True)
    b = dot_table(z[:, 256:512], axial[1], True)
    o = dot_table(z[:, 512:], axial[2], True)
    e = jnp.concatenate((a + b, a - b), axis=1)
    return e + o, e - o


def plane(recv_ref, c):
    return jnp.concatenate([recv_ref[a, :, c].reshape(256, 128) for a in range(8)], axis=1)


def put(z, axial, send_ref, group):
    for side, y in enumerate(backward(z, axial)):
        for a in range(4):
            for c in range(3):
                block = y[128 * c : 128 * c + 128, 128 * a : 128 * a + 128]
                send_ref[4 * side + a, :, 3 * group + c] = block.reshape(16, 8, 128)


def add_to(sum_ref, c, value):
    sum_ref[...] = jnp.where(c == 0, 0.0, sum_ref[...]) + value


def first_kernel(recv_ref, azimuth_ref, zero_ref, two_ref, odd_ref, out_ref, sum_ref):
    def step(c, _):
        axial = (parts(zero_ref), parts(two_ref), parts(odd_ref))
        azimuth = (azimuth_ref[0], azimuth_ref[1])
        y = forward(plane(recv_ref, c), azimuth, axial)
        out_ref[c] = y
        add_to(sum_ref, c, y)
        return _

    lax.fori_loop(0, 3, step, 0)


def second_kernel(
    recv_ref,
    own_ref,
    own_sum_ref,
    azimuth_ref,
    back_ref,
    zero_ref,
    two_ref,
    odd_ref,
    keep_ref,
    pass_ref,
    field_ref,
    sum_ref,
):
    def step(c, _):
        axial = (parts(zero_ref), parts(two_ref), parts(odd_ref))
        azimuth = (azimuth_ref[0], azimuth_ref[1])
        y = forward(plane(recv_ref, 3 + c), azimuth, axial)
        field_ref[c] = y
        add_to(sum_ref, c, y)
        return _

    lax.fori_loop(0, 3, step, 0)
    core = lax.axis_index("az") % 2

    def product(c, _):
        rhs = own_ref[c] * sum_ref[...] + field_ref[c] * own_sum_ref[...]
        side = []
        for parity in range(2):
            mine, theirs = back_ref[core, parity], back_ref[1 - core, parity]
            table = jnp.concatenate((mine[:64], theirs[:64], mine[64:], theirs[64:]), axis=0)
            side.append(table_dot(table, rhs[128 * parity : 128 * parity + 128]))
        upper, lower = side[0] + side[1], side[0] - side[1]
        keep_ref[c] = jnp.concatenate((upper[:64], lower[:64]), axis=0)
        pass_ref[c] = jnp.concatenate((upper[64:], lower[64:]), axis=0)
        return _

    lax.fori_loop(0, 3, product, 0)


def tangent_kernel(
    own_ref,
    own_sum_ref,
    other_ref,
    back_ref,
    zero_ref,
    two_ref,
    odd_ref,
    send_ref,
    sum_ref,
    turned_ref,
):
    core = lax.axis_index("az") % 2
    sum_ref[...] = other_ref[0] + other_ref[1] + other_ref[2]

    def step(c, _):
        rhs = own_ref[c] * sum_ref[...] + other_ref[c] * own_sum_ref[...]
        e = table_dot(back_ref[core, 0], rhs[:128])
        o = table_dot(back_ref[core, 1], rhs[128:])
        turned_ref[c] = jnp.concatenate((e + o, e - o), axis=0)
        return _

    lax.fori_loop(0, 3, step, 0)
    axial = (parts(zero_ref), parts(two_ref), parts(odd_ref))
    put(turned_ref[...].reshape(384, 1024), axial, send_ref, 0)


def join_kernel(tangent_ref, keep_ref, other_ref, zero_ref, two_ref, odd_ref, send_ref):
    send_ref[:, :, :3] = tangent_ref[...]
    z = keep_ref[...] + other_ref[...]
    put(z.reshape(384, 1024), (parts(zero_ref), parts(two_ref), parts(odd_ref)), send_ref, 1)


def gather_kernel(
    recv_ref, tangent_ref, second_ref, rate_ref, table_ref, out_ref, out2_ref, result_ref, scale_ref, sems
):
    radial = rate_ref.shape[0]
    azimuth_count, axial_count = 256, 1024
    axial = lax.axis_index("ax") * 128 + lax.broadcasted_iota(jnp.int32, (1, 128), 1)
    wave = jnp.minimum(axial, axial_count - axial).astype(F32) * axial_unit
    base = rate_ref[...] + wave * wave

    def scale(m, _):
        azimuth = lax.axis_index("az") * 16 + m
        wave_azimuth = jnp.minimum(azimuth, azimuth_count - azimuth).astype(F32)
        scale_ref[m] = 1.0 / (1.0 + viscosity * (base + wave_azimuth * wave_azimuth))
        return _

    lax.fori_loop(0, 16, scale, 0)
    outs = (out_ref, out2_ref)
    fields = (tangent_ref, second_ref)

    def give(which, c, core):
        place = (c, pl.ds(8 * core, 8))
        return pltpu.make_async_copy(
            result_ref.at[(which, *place)], outs[which].at[place], sems.at[which, c, core]
        )


    def step(c, _):
        for core in range(2):
            x = []
            for q in range(4):
                rows = [recv_ref[:, q, 2 * core + i, c] for i in range(2)]
                rows = jnp.concatenate(rows, axis=2)
                x.append(pltpu.roll(rows, 8 - 2 * q, 1) if q else rows)
            for p in range(4):
                y = table_dot(table_ref[p], pick(x, p, -1).reshape(128, 256))
                for n in range(2):
                    m = 8 * core + 2 * p + n
                    for which in range(2):
                        term = y[radial * n : radial * n + radial, 128 * which : 128 * which + 128]
                        value = (fields[which][c, m] + time_step * term) * scale_ref[m]
                        result_ref[which, c, m] = value
            for which in range(2):
                give(which, c, core).start(priority=which)
        return _

    lax.fori_loop(0, 3, step, 0)

    def finish(c, _):
        for which in range(2):
            for core in range(2):
                give(which, c, core).wait()
        return _

    lax.fori_loop(0, 3, finish, 0)


WHOLE = pl.BlockSpec(memory_space=pltpu.VMEM)
LEFT = pl.BlockSpec(memory_space=pl.ANY)


def call(kernel, shapes, *args, scratch=(), limit=24, specs=None, out_spec=WHOLE):
    out = [jax.ShapeDtypeStruct(shape, F32) for shape in shapes]
    return pl.pallas_call(
        kernel,
        out_shape=out,
        in_specs=specs or [WHOLE] * len(args),
        out_specs=[out_spec] * len(out),
        scratch_shapes=list(scratch),
        compiler_params=pltpu.CompilerParams(vmem_limit_bytes=limit * 1024 * 1024),
    )(*args)


def radial_tables(radial):
    t, b, n = np.meshgrid(np.arange(16), np.arange(4), np.arange(2), indexing="ij")
    there, back = [], []
    for p in range(4):
        j = (4 * t + (p - b) % 4).ravel()
        same = n.ravel()[:, None, None] == np.arange(2)[None, :, None]
        plain = np.where(same, radial[j][:, None, :], 0.0)
        high, low = halves(plain)
        none = np.zeros_like(low)
        rows = [np.stack(pair, axis=2).reshape(128, 256) for pair in ((high, high), (low, none))]
        there.append(np.concatenate(rows, axis=0))
        back.append(stacked(plain.reshape(128, 128).T))
    return np.stack(there), np.stack(back)


def body(saved_flow, saved_adjoint, tangent, second_adjoint, radial_rate):
    radial = radial_table(64)
    there, home_again = radial_tables(radial)
    half, quarter = np.arange(128), np.arange(256)
    azimuth = np.stack([stacked(hartley_table(2 * half + p, half, 256)) for p in range(2)])
    kept = [np.array([16 * a + 8 * s + i for a in range(8) for i in range(8)]) for s in range(2)]
    back = np.stack(
        [
            np.stack([stacked(hartley_table(rows, 2 * half + p, 256)) for p in range(2)])
            for rows in kept
        ]
    )
    axial = (
        halves(hartley_table(quarter, 4 * quarter, 1024)),
        halves(hartley_table(quarter, 4 * quarter + 2, 1024)),
        halves(hartley_table(np.arange(512), 2 * np.arange(512) + 1, 1024)),
    )
    rate = jnp.broadcast_to(radial_rate[:, None], (64, 128))
    pairs = [(i, i ^ 1) for i in range(16)]
    grid, rows = (256, 1024), (128, 1024)

    def swap(x):
        return lax.ppermute(x, "az", pairs)

    def whole(x):
        return lax.all_to_all(x, ("ax", "az"), 0, 0, tiled=True)

    (spread,) = call(
        spread_kernel,
        [(16, 4, 4, 3, 16, 128)],
        *(
            pltpu.with_memory_space_constraint(x, pltpu.HBM)
            for x in (saved_flow, tangent, second_adjoint, saved_adjoint)
        ),
        pltpu.with_memory_space_constraint(jnp.asarray(there), pltpu.HBM),
        scratch=(
            pltpu.VMEM((4, 256, 256), BF16),
            pltpu.VMEM((4, 3, 16, 64, 128), F32),
            pltpu.SemaphoreType.DMA,
            pltpu.SemaphoreType.DMA((4, 6)),
        ),
        specs=[LEFT] * 5,
    )
    recv = whole(spread.reshape(128, 6, 16, 128)).reshape(8, 16, 6, 16, 128)
    own, own_sum = call(first_kernel, [(3, *grid), grid], recv, azimuth, *axial)
    other = swap(own)
    keep, passed = call(
        second_kernel,
        [(3, *rows)] * 2,
        recv,
        own,
        own_sum,
        azimuth,
        back,
        *axial,
        scratch=(pltpu.VMEM((3, *grid), F32), pltpu.VMEM(grid, F32)),
    )
    joined = swap(passed)
    (turned,) = call(
        tangent_kernel,
        [(8, 16, 3, 8, 128)],
        own,
        own_sum,
        other,
        back,
        *axial,
        scratch=(pltpu.VMEM(grid, F32), pltpu.VMEM((3, *rows), F32)),
    )
    (send,) = call(join_kernel, [(8, 16, 6, 8, 128)], turned, keep, joined, *axial)
    home = whole(send.reshape(128, 6, 8, 128)).reshape(16, 4, 4, 3, 8, 128)
    shape = tangent.shape
    return tuple(
        call(
            gather_kernel,
            [shape, shape],
            home,
            tangent,
            second_adjoint,
            rate,
            home_again,
            scratch=(
                pltpu.VMEM((2, *shape), F32),
                pltpu.VMEM(shape[1:], F32),
                pltpu.SemaphoreType.DMA((2, 3, 2)),
            ),
            out_spec=LEFT,
        )
    )


def solution(mesh):
    spec = P(None, "az", None, "ax")
    return jax.shard_map(
        body, mesh=mesh, in_specs=(spec,) * 4 + (P(),), out_specs=(spec, spec), check_vma=False
    )
```

```python
import math

import jax
import jax.numpy as jnp
import numpy as np
from jax import lax
from jax.experimental import pallas as pl
from jax.experimental.pallas import tpu as pltpu
from jax.sharding import PartitionSpec as P

time_step = 0.1
viscosity = 0.005
axial_unit = 2.0 * math.pi / 20.0
F32 = jnp.float32
BF16 = jnp.bfloat16


def radial_table(count):
    points = np.arange(count)[:, None]
    orders = np.arange(count)[None, :]
    phases = orders * (2 * points + 1) % (4 * count)
    scales = np.where(orders == 0, math.sqrt(1.0 / count), math.sqrt(2.0 / count))
    return np.cos(phases * (math.pi / (2.0 * count))) * scales


def hartley_table(rows, cols, length):
    angles = (rows[:, None] * cols[None, :] % length) * (2.0 * math.pi / length)
    return (np.cos(angles) + np.sin(angles)) / math.sqrt(length)


def halves(table):
    table = np.asarray(table, np.float32)
    high = table.astype(BF16)
    low = (table - high.astype(np.float32)).astype(BF16)
    return np.stack((high, low))


def split(x):
    high = x.astype(BF16)
    return high, (x - high.astype(F32)).astype(BF16)


def stacked(table):
    high, low = halves(table)
    return np.block([[high, high], [low, np.zeros_like(low)]])


def lay(high, low):
    right = jnp.concatenate((high, jnp.zeros_like(low)), axis=0)
    return jnp.concatenate((jnp.concatenate((high, low), axis=0), right), axis=1)


def table_dot(table, x):
    out = jnp.dot(table, jnp.concatenate(split(x), axis=0), preferred_element_type=F32)
    half = out.shape[0] // 2
    return out[:half] + out[half:]


def dot_table(x, table, turned):
    high, low = split(x)
    left = jnp.concatenate((high, low, high), axis=1)
    right = jnp.concatenate((table[0], table[0], table[1]), axis=1 if turned else 0)
    return lax.dot_general(
        left, right, (((1,), (1 if turned else 0,)), ((), ())), preferred_element_type=F32
    )


def parts(ref):
    return ref[0], ref[1]


def pick(arrays, first, step):
    block = lax.broadcasted_iota(jnp.int32, arrays[0].shape, 1) // 2
    out = arrays[first % 4]
    for b in range(1, 4):
        out = jnp.where(block == b, arrays[(first + step * b) % 4], out)
    return out


def spread_kernel(
    flow_ref,
    tangent_ref,
    second_ref,
    adjoint_ref,
    radial_ref,
    out_ref,
    table_ref,
    field_ref,
    sem,
    sems,
):
    fetch_table = pltpu.make_async_copy(radial_ref, table_ref, sem)

    def fetch(i, ref, step):
        c, start = step // 2, pl.multiple_of(step % 2 * 8, 8)
        place = (c, pl.ds(start, 8))
        return pltpu.make_async_copy(ref.at[place], field_ref.at[(i, *place)], sems.at[i, step])

    fields = tuple(enumerate((flow_ref, second_ref, tangent_ref, adjoint_ref)))
    for step in range(6):
        for i, ref in fields:
            fetch(i, ref, step).start(priority=i % 2)
        if step == 0:
            fetch_table.start()
    fetch_table.wait()

    def work(c, _):
        for step in (2 * c, 2 * c + 1):
            for i, ref in fields:
                fetch(i, ref, step).wait()
        for start in (0, 8):
            y = []
            for p in range(4):
                x = []
                for m in (start + 2 * p, start + 2 * p + 1):
                    x.extend(split(jnp.concatenate([field_ref[i, c, m] for i in range(4)], axis=1)))
                out = jnp.dot(
                    table_ref[p], jnp.concatenate(x, axis=0), preferred_element_type=F32
                )
                y.append((out[:128] + out[128:]).reshape(16, 8, 512))
            for q in range(4):
                z = pick(y, q, 1)
                z = pltpu.roll(z, 2 * q, 1) if q else z
                for i in range(4):
                    out_ref[:, q, i, c, start : start + 8, :] = z[:, :, 128 * i : 128 * i + 128]
        return _

    lax.fori_loop(0, 3, work, 0)


def forward(x, azimuth, axial):
    y = jnp.concatenate(
        (table_dot(azimuth[0], x[:128] + x[128:]), table_dot(azimuth[1], x[:128] - x[128:])), axis=0
    )
    s = y[:, :512] + y[:, 512:]
    d = y[:, :512] - y[:, 512:]
    return jnp.concatenate(
        (
            dot_table(s[:, :256] + s[:, 256:], axial[0], False),
            dot_table(s[:, :256] - s[:, 256:], axial[1], False),
            dot_table(d, axial[2], False),
        ),
        axis=1,
    )


def backward(z, axial):
    a = dot_table(z[:, :256], axial[0], True)
    b = dot_table(z[:, 256:512], axial[1], True)
    o = dot_table(z[:, 512:], axial[2], True)
    e = jnp.concatenate((a + b, a - b), axis=1)
    return e + o, e - o


def plane(recv_ref, c):
    return jnp.concatenate([recv_ref[a, :, c].reshape(256, 128) for a in range(8)], axis=1)


def put(z, axial, send_ref, group):
    for side, y in enumerate(backward(z, axial)):
        for a in range(4):
            for c in range(3):
                block = y[128 * c : 128 * c + 128, 128 * a : 128 * a + 128]
                send_ref[4 * side + a, :, 3 * group + c] = block.reshape(16, 8, 128)


def add_to(sum_ref, c, value):
    sum_ref[...] = jnp.where(c == 0, 0.0, sum_ref[...]) + value


def first_kernel(recv_ref, azimuth_ref, zero_ref, two_ref, odd_ref, out_ref, sum_ref):
    def step(c, _):
        axial = (parts(zero_ref), parts(two_ref), parts(odd_ref))
        azimuth = tuple(lay(*parts(azimuth_ref.at[p])) for p in range(2))
        y = forward(plane(recv_ref, c), azimuth, axial)
        out_ref[c] = y
        add_to(sum_ref, c, y)
        return _

    lax.fori_loop(0, 3, step, 0)


def second_kernel(
    recv_ref,
    own_ref,
    own_sum_ref,
    azimuth_ref,
    back_ref,
    zero_ref,
    two_ref,
    odd_ref,
    keep_ref,
    pass_ref,
    field_ref,
    sum_ref,
):
    def step(c, _):
        axial = (parts(zero_ref), parts(two_ref), parts(odd_ref))
        azimuth = tuple(lay(*parts(azimuth_ref.at[p])) for p in range(2))
        y = forward(plane(recv_ref, 3 + c), azimuth, axial)
        field_ref[c] = y
        add_to(sum_ref, c, y)
        return _

    lax.fori_loop(0, 3, step, 0)
    core = lax.axis_index("az") % 2

    def product(c, _):
        rhs = own_ref[c] * sum_ref[...] + field_ref[c] * own_sum_ref[...]
        side = []
        for parity in range(2):
            mine, theirs = back_ref.at[core, parity], back_ref.at[1 - core, parity]
            table = lay(*(jnp.concatenate((mine[i], theirs[i]), axis=0) for i in range(2)))
            side.append(table_dot(table, rhs[128 * parity : 128 * parity + 128]))
        upper, lower = side[0] + side[1], side[0] - side[1]
        keep_ref[c] = jnp.concatenate((upper[:64], lower[:64]), axis=0)
        pass_ref[c] = jnp.concatenate((upper[64:], lower[64:]), axis=0)
        return _

    lax.fori_loop(0, 3, product, 0)


def tangent_kernel(
    own_ref,
    own_sum_ref,
    other_ref,
    back_ref,
    zero_ref,
    two_ref,
    odd_ref,
    send_ref,
    sum_ref,
    turned_ref,
):
    core = lax.axis_index("az") % 2
    sum_ref[...] = other_ref[0] + other_ref[1] + other_ref[2]

    def step(c, _):
        rhs = own_ref[c] * sum_ref[...] + other_ref[c] * own_sum_ref[...]
        e = table_dot(lay(*parts(back_ref.at[core, 0])), rhs[:128])
        o = table_dot(lay(*parts(back_ref.at[core, 1])), rhs[128:])
        turned_ref[c] = jnp.concatenate((e + o, e - o), axis=0)
        return _

    lax.fori_loop(0, 3, step, 0)
    axial = (parts(zero_ref), parts(two_ref), parts(odd_ref))
    put(turned_ref[...].reshape(384, 1024), axial, send_ref, 0)


def join_kernel(tangent_ref, keep_ref, other_ref, zero_ref, two_ref, odd_ref, send_ref):
    send_ref[:, :, :3] = tangent_ref[...]
    z = keep_ref[...] + other_ref[...]
    put(z.reshape(384, 1024), (parts(zero_ref), parts(two_ref), parts(odd_ref)), send_ref, 1)


def gather_kernel(
    recv_ref, tangent_ref, second_ref, rate_ref, table_ref, out_ref, out2_ref, result_ref, scale_ref, sems
):
    radial = rate_ref.shape[0]
    azimuth_count, axial_count = 256, 1024
    axial = lax.axis_index("ax") * 128 + lax.broadcasted_iota(jnp.int32, (1, 128), 1)
    wave = jnp.minimum(axial, axial_count - axial).astype(F32) * axial_unit
    base = rate_ref[...] + wave * wave

    def scale(m, _):
        azimuth = lax.axis_index("az") * 16 + m
        wave_azimuth = jnp.minimum(azimuth, azimuth_count - azimuth).astype(F32)
        scale_ref[m] = 1.0 / (1.0 + viscosity * (base + wave_azimuth * wave_azimuth))
        return _

    lax.fori_loop(0, 16, scale, 0)
    outs = (out_ref, out2_ref)
    fields = (tangent_ref, second_ref)

    def give(which, c, core):
        place = (c, pl.ds(8 * core, 8))
        return pltpu.make_async_copy(
            result_ref.at[(which, *place)], outs[which].at[place], sems.at[which, c, core]
        )


    def step(c, _):
        for core in range(2):
            x = []
            for q in range(4):
                rows = [recv_ref[:, q, 2 * core + i, c] for i in range(2)]
                rows = jnp.concatenate(rows, axis=2)
                x.append(pltpu.roll(rows, 8 - 2 * q, 1) if q else rows)
            for p in range(4):
                y = table_dot(table_ref[p], pick(x, p, -1).reshape(128, 256))
                for n in range(2):
                    m = 8 * core + 2 * p + n
                    for which in range(2):
                        term = y[radial * n : radial * n + radial, 128 * which : 128 * which + 128]
                        value = (fields[which][c, m] + time_step * term) * scale_ref[m]
                        result_ref[which, c, m] = value
            for which in range(2):
                give(which, c, core).start(priority=which)
        return _

    lax.fori_loop(0, 3, step, 0)

    def finish(c, _):
        for which in range(2):
            for core in range(2):
                give(which, c, core).wait()
        return _

    lax.fori_loop(0, 3, finish, 0)


WHOLE = pl.BlockSpec(memory_space=pltpu.VMEM)
LEFT = pl.BlockSpec(memory_space=pl.ANY)


def call(kernel, shapes, *args, scratch=(), limit=24, specs=None, out_spec=WHOLE):
    out = [jax.ShapeDtypeStruct(shape, F32) for shape in shapes]
    return pl.pallas_call(
        kernel,
        out_shape=out,
        in_specs=specs or [WHOLE] * len(args),
        out_specs=[out_spec] * len(out),
        scratch_shapes=list(scratch),
        compiler_params=pltpu.CompilerParams(vmem_limit_bytes=limit * 1024 * 1024),
    )(*args)


def radial_tables(radial):
    t, b, n = np.meshgrid(np.arange(16), np.arange(4), np.arange(2), indexing="ij")
    there, back = [], []
    for p in range(4):
        j = (4 * t + (p - b) % 4).ravel()
        same = n.ravel()[:, None, None] == np.arange(2)[None, :, None]
        plain = np.where(same, radial[j][:, None, :], 0.0)
        high, low = halves(plain)
        none = np.zeros_like(low)
        rows = [np.stack(pair, axis=2).reshape(128, 256) for pair in ((high, high), (low, none))]
        there.append(np.concatenate(rows, axis=0))
        back.append(stacked(plain.reshape(128, 128).T))
    return np.stack(there), np.stack(back)


def body(saved_flow, saved_adjoint, tangent, second_adjoint, radial_rate):
    radial = radial_table(64)
    there, home_again = radial_tables(radial)
    half, quarter = np.arange(128), np.arange(256)
    azimuth = np.stack([halves(hartley_table(2 * half + p, half, 256)) for p in range(2)])
    kept = [np.array([16 * a + 8 * s + i for a in range(8) for i in range(8)]) for s in range(2)]
    back = np.stack(
        [
            np.stack([halves(hartley_table(rows, 2 * half + p, 256)) for p in range(2)])
            for rows in kept
        ]
    )
    axial = (
        halves(hartley_table(quarter, 4 * quarter, 1024)),
        halves(hartley_table(quarter, 4 * quarter + 2, 1024)),
        halves(hartley_table(np.arange(512), 2 * np.arange(512) + 1, 1024)),
    )
    rate = jnp.broadcast_to(radial_rate[:, None], (64, 128))
    pairs = [(i, i ^ 1) for i in range(16)]
    grid, rows = (256, 1024), (128, 1024)

    def swap(x):
        return lax.ppermute(x, "az", pairs)

    def whole(x):
        return lax.all_to_all(x, ("ax", "az"), 0, 0, tiled=True)

    (spread,) = call(
        spread_kernel,
        [(16, 4, 4, 3, 16, 128)],
        *(
            pltpu.with_memory_space_constraint(x, pltpu.HBM)
            for x in (saved_flow, tangent, second_adjoint, saved_adjoint)
        ),
        pltpu.with_memory_space_constraint(jnp.asarray(there), pltpu.HBM),
        scratch=(
            pltpu.VMEM((4, 256, 256), BF16),
            pltpu.VMEM((4, 3, 16, 64, 128), F32),
            pltpu.SemaphoreType.DMA,
            pltpu.SemaphoreType.DMA((4, 6)),
        ),
        specs=[LEFT] * 5,
    )
    recv = whole(spread.reshape(128, 6, 16, 128)).reshape(8, 16, 6, 16, 128)
    own, own_sum = call(first_kernel, [(3, *grid), grid], recv, azimuth, *axial)
    other = swap(own)
    keep, passed = call(
        second_kernel,
        [(3, *rows)] * 2,
        recv,
        own,
        own_sum,
        azimuth,
        back,
        *axial,
        scratch=(pltpu.VMEM((3, *grid), F32), pltpu.VMEM(grid, F32)),
    )
    joined = swap(passed)
    (turned,) = call(
        tangent_kernel,
        [(8, 16, 3, 8, 128)],
        own,
        own_sum,
        other,
        back,
        *axial,
        scratch=(pltpu.VMEM(grid, F32), pltpu.VMEM((3, *rows), F32)),
    )
    (send,) = call(join_kernel, [(8, 16, 6, 8, 128)], turned, keep, joined, *axial)
    home = whole(send.reshape(128, 6, 8, 128)).reshape(16, 4, 4, 3, 8, 128)
    shape = tangent.shape
    return tuple(
        call(
            gather_kernel,
            [shape, shape],
            home,
            tangent,
            second_adjoint,
            rate,
            home_again,
            scratch=(
                pltpu.VMEM((2, *shape), F32),
                pltpu.VMEM(shape[1:], F32),
                pltpu.SemaphoreType.DMA((2, 3, 2)),
            ),
            out_spec=LEFT,
        )
    )


def solution(mesh):
    spec = P(None, "az", None, "ax")
    return jax.shard_map(
        body, mesh=mesh, in_specs=(spec,) * 4 + (P(),), out_specs=(spec, spec), check_vma=False
    )
```

```python
import math

import jax
import jax.numpy as jnp
import numpy as np
from jax import lax
from jax.experimental import pallas as pl
from jax.experimental.pallas import tpu as pltpu
from jax.sharding import PartitionSpec as P

time_step = 0.1
viscosity = 0.005
axial_unit = 2.0 * math.pi / 20.0
F32 = jnp.float32
BF16 = jnp.bfloat16


def radial_table(count):
    points = np.arange(count)[:, None]
    orders = np.arange(count)[None, :]
    phases = orders * (2 * points + 1) % (4 * count)
    scales = np.where(orders == 0, math.sqrt(1.0 / count), math.sqrt(2.0 / count))
    return np.cos(phases * (math.pi / (2.0 * count))) * scales


def hartley_table(rows, cols, length):
    angles = (rows[:, None] * cols[None, :] % length) * (2.0 * math.pi / length)
    return (np.cos(angles) + np.sin(angles)) / math.sqrt(length)


def halves(table):
    table = np.asarray(table, np.float32)
    high = table.astype(BF16)
    low = (table - high.astype(np.float32)).astype(BF16)
    return np.stack((high, low))


def split(x):
    high = x.astype(BF16)
    return high, (x - high.astype(F32)).astype(BF16)


def stacked(table):
    high, low = halves(table)
    return np.block([[high, high], [low, np.zeros_like(low)]])


def lay(high, low):
    right = jnp.concatenate((high, jnp.zeros_like(low)), axis=0)
    return jnp.concatenate((jnp.concatenate((high, low), axis=0), right), axis=1)


def table_dot(table, x):
    out = jnp.dot(table, jnp.concatenate(split(x), axis=0), preferred_element_type=F32)
    half = out.shape[0] // 2
    return out[:half] + out[half:]


def dot_table(x, table, turned):
    high, low = split(x)
    numbers = (((1,), (1 if turned else 0,)), ((), ()))
    both = lax.dot_general(
        jnp.concatenate((high, low), axis=0), table[0], numbers, preferred_element_type=F32
    )
    rest = lax.dot_general(high, table[1], numbers, preferred_element_type=F32)
    return both[: x.shape[0]] + both[x.shape[0] :] + rest


def parts(ref):
    return ref[0], ref[1]


def pick(arrays, first, step):
    block = lax.broadcasted_iota(jnp.int32, arrays[0].shape, 1) // 2
    out = arrays[first % 4]
    for b in range(1, 4):
        out = jnp.where(block == b, arrays[(first + step * b) % 4], out)
    return out


def spread_kernel(
    flow_ref,
    tangent_ref,
    second_ref,
    adjoint_ref,
    radial_ref,
    out_ref,
    table_ref,
    field_ref,
    sem,
    sems,
):
    fetch_table = pltpu.make_async_copy(radial_ref, table_ref, sem)

    def fetch(i, ref, c):
        return pltpu.make_async_copy(ref.at[c], field_ref.at[i, c], sems.at[i, c])

    fields = tuple(enumerate((flow_ref, second_ref, tangent_ref, adjoint_ref)))
    for c in range(3):
        for i, ref in fields:
            fetch(i, ref, c).start(priority=i % 2)
        if c == 0:
            fetch_table.start()
    fetch_table.wait()

    def work(c, _):
        for i, ref in fields:
            fetch(i, ref, c).wait()
        for start in (0, 8):
            y = []
            for p in range(4):
                x = []
                for m in (start + 2 * p, start + 2 * p + 1):
                    x.extend(split(jnp.concatenate([field_ref[i, c, m] for i in range(4)], axis=1)))
                out = jnp.dot(
                    table_ref[p], jnp.concatenate(x, axis=0), preferred_element_type=F32
                )
                y.append((out[:128] + out[128:]).reshape(16, 8, 512))
            for q in range(4):
                z = pick(y, q, 1)
                z = pltpu.roll(z, 2 * q, 1) if q else z
                for i in range(4):
                    out_ref[:, q, i, c, start : start + 8, :] = z[:, :, 128 * i : 128 * i + 128]
        return _

    lax.fori_loop(0, 3, work, 0)


def forward(x, azimuth, axial):
    y = jnp.concatenate(
        (table_dot(azimuth[0], x[:128] + x[128:]), table_dot(azimuth[1], x[:128] - x[128:])), axis=0
    )
    s = y[:, :512] + y[:, 512:]
    d = y[:, :512] - y[:, 512:]
    return jnp.concatenate(
        (
            dot_table(s[:, :256] + s[:, 256:], axial[0], False),
            dot_table(s[:, :256] - s[:, 256:], axial[1], False),
            dot_table(d, axial[2], False),
        ),
        axis=1,
    )


def backward(z, axial):
    a = dot_table(z[:, :256], axial[0], True)
    b = dot_table(z[:, 256:512], axial[1], True)
    o = dot_table(z[:, 512:], axial[2], True)
    e = jnp.concatenate((a + b, a - b), axis=1)
    return e + o, e - o


def plane(recv_ref, c):
    return jnp.concatenate([recv_ref[a, :, c].reshape(256, 128) for a in range(8)], axis=1)


def put(z, axial, send_ref, group):
    for side, y in enumerate(backward(z, axial)):
        for a in range(4):
            for c in range(3):
                block = y[128 * c : 128 * c + 128, 128 * a : 128 * a + 128]
                send_ref[4 * side + a, :, 3 * group + c] = block.reshape(16, 8, 128)


def add_to(sum_ref, c, value):
    sum_ref[...] = jnp.where(c == 0, 0.0, sum_ref[...]) + value


def first_kernel(recv_ref, azimuth_ref, zero_ref, two_ref, odd_ref, out_ref, sum_ref):
    def step(c, _):
        axial = (parts(zero_ref), parts(two_ref), parts(odd_ref))
        azimuth = tuple(lay(*parts(azimuth_ref.at[p])) for p in range(2))
        y = forward(plane(recv_ref, c), azimuth, axial)
        out_ref[c] = y
        add_to(sum_ref, c, y)
        return _

    lax.fori_loop(0, 3, step, 0)


def second_kernel(
    recv_ref,
    own_ref,
    own_sum_ref,
    azimuth_ref,
    back_ref,
    zero_ref,
    two_ref,
    odd_ref,
    keep_ref,
    pass_ref,
    field_ref,
    sum_ref,
):
    def step(c, _):
        axial = (parts(zero_ref), parts(two_ref), parts(odd_ref))
        azimuth = tuple(lay(*parts(azimuth_ref.at[p])) for p in range(2))
        y = forward(plane(recv_ref, 3 + c), azimuth, axial)
        field_ref[c] = y
        add_to(sum_ref, c, y)
        return _

    lax.fori_loop(0, 3, step, 0)
    core = lax.axis_index("az") % 2

    def product(c, _):
        rhs = own_ref[c] * sum_ref[...] + field_ref[c] * own_sum_ref[...]
        side = []
        for parity in range(2):
            mine, theirs = back_ref.at[core, parity], back_ref.at[1 - core, parity]
            table = lay(*(jnp.concatenate((mine[i], theirs[i]), axis=0) for i in range(2)))
            side.append(table_dot(table, rhs[128 * parity : 128 * parity + 128]))
        upper, lower = side[0] + side[1], side[0] - side[1]
        keep_ref[c] = jnp.concatenate((upper[:64], lower[:64]), axis=0)
        pass_ref[c] = jnp.concatenate((upper[64:], lower[64:]), axis=0)
        return _

    lax.fori_loop(0, 3, product, 0)


def tangent_kernel(
    own_ref,
    own_sum_ref,
    other_ref,
    back_ref,
    zero_ref,
    two_ref,
    odd_ref,
    send_ref,
    sum_ref,
    turned_ref,
):
    core = lax.axis_index("az") % 2
    sum_ref[...] = other_ref[0] + other_ref[1] + other_ref[2]

    def step(c, _):
        rhs = own_ref[c] * sum_ref[...] + other_ref[c] * own_sum_ref[...]
        e = table_dot(lay(*parts(back_ref.at[core, 0])), rhs[:128])
        o = table_dot(lay(*parts(back_ref.at[core, 1])), rhs[128:])
        turned_ref[c] = jnp.concatenate((e + o, e - o), axis=0)
        return _

    lax.fori_loop(0, 3, step, 0)
    axial = (parts(zero_ref), parts(two_ref), parts(odd_ref))
    put(turned_ref[...].reshape(384, 1024), axial, send_ref, 0)


def join_kernel(tangent_ref, keep_ref, other_ref, zero_ref, two_ref, odd_ref, send_ref):
    send_ref[:, :, :3] = tangent_ref[...]
    z = keep_ref[...] + other_ref[...]
    put(z.reshape(384, 1024), (parts(zero_ref), parts(two_ref), parts(odd_ref)), send_ref, 1)


def gather_kernel(
    recv_ref, tangent_ref, second_ref, rate_ref, table_ref, out_ref, out2_ref, result_ref, scale_ref, sems
):
    radial = rate_ref.shape[0]
    azimuth_count, axial_count = 256, 1024
    axial = lax.axis_index("ax") * 128 + lax.broadcasted_iota(jnp.int32, (1, 128), 1)
    wave = jnp.minimum(axial, axial_count - axial).astype(F32) * axial_unit
    base = rate_ref[...] + wave * wave

    def scale(m, _):
        azimuth = lax.axis_index("az") * 16 + m
        wave_azimuth = jnp.minimum(azimuth, azimuth_count - azimuth).astype(F32)
        scale_ref[m] = 1.0 / (1.0 + viscosity * (base + wave_azimuth * wave_azimuth))
        return _

    lax.fori_loop(0, 16, scale, 0)
    outs = (out_ref, out2_ref)
    fields = (tangent_ref, second_ref)

    def give(which, c, core):
        place = (c, pl.ds(8 * core, 8))
        return pltpu.make_async_copy(
            result_ref.at[(which, *place)], outs[which].at[place], sems.at[which, c, core]
        )


    def step(c, _):
        for core in range(2):
            x = []
            for q in range(4):
                rows = [recv_ref[:, q, 2 * core + i, c] for i in range(2)]
                rows = jnp.concatenate(rows, axis=2)
                x.append(pltpu.roll(rows, 8 - 2 * q, 1) if q else rows)
            for p in range(4):
                y = table_dot(table_ref[p], pick(x, p, -1).reshape(128, 256))
                for n in range(2):
                    m = 8 * core + 2 * p + n
                    for which in range(2):
                        term = y[radial * n : radial * n + radial, 128 * which : 128 * which + 128]
                        value = (fields[which][c, m] + time_step * term) * scale_ref[m]
                        result_ref[which, c, m] = value
            for which in range(2):
                give(which, c, core).start(priority=which)
        return _

    lax.fori_loop(0, 3, step, 0)

    def finish(c, _):
        for which in range(2):
            for core in range(2):
                give(which, c, core).wait()
        return _

    lax.fori_loop(0, 3, finish, 0)


WHOLE = pl.BlockSpec(memory_space=pltpu.VMEM)
LEFT = pl.BlockSpec(memory_space=pl.ANY)


def call(kernel, shapes, *args, scratch=(), limit=24, specs=None, out_spec=WHOLE):
    out = [jax.ShapeDtypeStruct(shape, F32) for shape in shapes]
    return pl.pallas_call(
        kernel,
        out_shape=out,
        in_specs=specs or [WHOLE] * len(args),
        out_specs=[out_spec] * len(out),
        scratch_shapes=list(scratch),
        compiler_params=pltpu.CompilerParams(vmem_limit_bytes=limit * 1024 * 1024),
    )(*args)


def radial_tables(radial):
    t, b, n = np.meshgrid(np.arange(16), np.arange(4), np.arange(2), indexing="ij")
    there, back = [], []
    for p in range(4):
        j = (4 * t + (p - b) % 4).ravel()
        same = n.ravel()[:, None, None] == np.arange(2)[None, :, None]
        plain = np.where(same, radial[j][:, None, :], 0.0)
        high, low = halves(plain)
        none = np.zeros_like(low)
        rows = [np.stack(pair, axis=2).reshape(128, 256) for pair in ((high, high), (low, none))]
        there.append(np.concatenate(rows, axis=0))
        back.append(stacked(plain.reshape(128, 128).T))
    return np.stack(there), np.stack(back)


def body(saved_flow, saved_adjoint, tangent, second_adjoint, radial_rate):
    radial = radial_table(64)
    there, home_again = radial_tables(radial)
    half, quarter = np.arange(128), np.arange(256)
    azimuth = np.stack([halves(hartley_table(2 * half + p, half, 256)) for p in range(2)])
    kept = [np.array([16 * a + 8 * s + i for a in range(8) for i in range(8)]) for s in range(2)]
    back = np.stack(
        [
            np.stack([halves(hartley_table(rows, 2 * half + p, 256)) for p in range(2)])
            for rows in kept
        ]
    )
    axial = (
        halves(hartley_table(quarter, 4 * quarter, 1024)),
        halves(hartley_table(quarter, 4 * quarter + 2, 1024)),
        halves(hartley_table(np.arange(512), 2 * np.arange(512) + 1, 1024)),
    )
    rate = jnp.broadcast_to(radial_rate[:, None], (64, 128))
    pairs = [(i, i ^ 1) for i in range(16)]
    grid, rows = (256, 1024), (128, 1024)

    def swap(x):
        return lax.ppermute(x, "az", pairs)

    def whole(x):
        return lax.all_to_all(x, ("ax", "az"), 0, 0, tiled=True)

    (spread,) = call(
        spread_kernel,
        [(16, 4, 4, 3, 16, 128)],
        *(
            pltpu.with_memory_space_constraint(x, pltpu.HBM)
            for x in (saved_flow, tangent, second_adjoint, saved_adjoint)
        ),
        pltpu.with_memory_space_constraint(jnp.asarray(there), pltpu.HBM),
        scratch=(
            pltpu.VMEM((4, 256, 256), BF16),
            pltpu.VMEM((4, 3, 16, 64, 128), F32),
            pltpu.SemaphoreType.DMA,
            pltpu.SemaphoreType.DMA((4, 3)),
        ),
        specs=[LEFT] * 5,
    )
    recv = whole(spread.reshape(128, 6, 16, 128)).reshape(8, 16, 6, 16, 128)
    own, own_sum = call(first_kernel, [(3, *grid), grid], recv, azimuth, *axial)
    other = swap(own)
    keep, passed = call(
        second_kernel,
        [(3, *rows)] * 2,
        recv,
        own,
        own_sum,
        azimuth,
        back,
        *axial,
        scratch=(pltpu.VMEM((3, *grid), F32), pltpu.VMEM(grid, F32)),
    )
    joined = swap(passed)
    (turned,) = call(
        tangent_kernel,
        [(8, 16, 3, 8, 128)],
        own,
        own_sum,
        other,
        back,
        *axial,
        scratch=(pltpu.VMEM(grid, F32), pltpu.VMEM((3, *rows), F32)),
    )
    (send,) = call(join_kernel, [(8, 16, 6, 8, 128)], turned, keep, joined, *axial)
    home = whole(send.reshape(128, 6, 8, 128)).reshape(16, 4, 4, 3, 8, 128)
    shape = tangent.shape
    return tuple(
        call(
            gather_kernel,
            [shape, shape],
            home,
            tangent,
            second_adjoint,
            rate,
            home_again,
            scratch=(
                pltpu.VMEM((2, *shape), F32),
                pltpu.VMEM(shape[1:], F32),
                pltpu.SemaphoreType.DMA((2, 3, 2)),
            ),
            out_spec=LEFT,
        )
    )


def solution(mesh):
    spec = P(None, "az", None, "ax")
    return jax.shard_map(
        body, mesh=mesh, in_specs=(spec,) * 4 + (P(),), out_specs=(spec, spec), check_vma=False
    )
```

```python
import math

import jax
import jax.numpy as jnp
import numpy as np
from jax import lax
from jax.experimental import pallas as pl
from jax.experimental.pallas import tpu as pltpu
from jax.sharding import PartitionSpec as P

time_step = 0.1
viscosity = 0.005
axial_unit = 2.0 * math.pi / 20.0
F32 = jnp.float32
BF16 = jnp.bfloat16


def radial_table(count):
    points = np.arange(count)[:, None]
    orders = np.arange(count)[None, :]
    phases = orders * (2 * points + 1) % (4 * count)
    scales = np.where(orders == 0, math.sqrt(1.0 / count), math.sqrt(2.0 / count))
    return np.cos(phases * (math.pi / (2.0 * count))) * scales


def hartley_table(rows, cols, length):
    angles = (rows[:, None] * cols[None, :] % length) * (2.0 * math.pi / length)
    return (np.cos(angles) + np.sin(angles)) / math.sqrt(length)


def halves(table):
    table = np.asarray(table, np.float32)
    high = table.astype(BF16)
    low = (table - high.astype(np.float32)).astype(BF16)
    return np.stack((high, low))


def split(x):
    high = x.astype(BF16)
    return high, (x - high.astype(F32)).astype(BF16)


def stacked(table):
    high, low = halves(table)
    return np.block([[high, high], [low, np.zeros_like(low)]])


def lay(high, low):
    right = jnp.concatenate((high, jnp.zeros_like(low)), axis=0)
    return jnp.concatenate((jnp.concatenate((high, low), axis=0), right), axis=1)


def table_dot(table, x):
    out = jnp.dot(table, jnp.concatenate(split(x), axis=0), preferred_element_type=F32)
    half = out.shape[0] // 2
    return out[:half] + out[half:]


def dot_table(x, table, turned):
    high, low = split(x)
    numbers = (((1,), (1 if turned else 0,)), ((), ()))
    both = lax.dot_general(
        jnp.concatenate((high, low), axis=0), table[0], numbers, preferred_element_type=F32
    )
    rest = lax.dot_general(high, table[1], numbers, preferred_element_type=F32)
    return both[: x.shape[0]] + both[x.shape[0] :] + rest


def parts(ref):
    return ref[0], ref[1]


def pick(arrays, first, step):
    block = lax.broadcasted_iota(jnp.int32, arrays[0].shape, 1) // 2
    out = arrays[first % 4]
    for b in range(1, 4):
        out = jnp.where(block == b, arrays[(first + step * b) % 4], out)
    return out


def spread_kernel(
    flow_ref,
    tangent_ref,
    second_ref,
    adjoint_ref,
    radial_ref,
    out_ref,
    table_ref,
    field_ref,
    sem,
    sems,
):
    fetch_table = pltpu.make_async_copy(radial_ref, table_ref, sem)

    def fetch(i, ref, c, start):
        place = (c, pl.ds(start, 8))
        return pltpu.make_async_copy(
            ref.at[place], field_ref.at[(i, *place)], sems.at[i, c, start // 8]
        )

    fields = tuple(enumerate((flow_ref, second_ref, tangent_ref, adjoint_ref)))
    for c in range(3):
        for start in (0, 8):
            for i, ref in fields:
                fetch(i, ref, c, start).start(priority=i % 2)
            if c == start == 0:
                fetch_table.start()
    fetch_table.wait()

    def work(*groups):
        for place in groups:
            for i, ref in fields:
                fetch(i, ref, *place).wait()
        for c, start in groups:
            y = []
            for p in range(4):
                x = []
                for m in (start + 2 * p, start + 2 * p + 1):
                    x.extend(split(jnp.concatenate([field_ref[i, c, m] for i in range(4)], axis=1)))
                out = jnp.dot(
                    table_ref[p], jnp.concatenate(x, axis=0), preferred_element_type=F32
                )
                y.append((out[:128] + out[128:]).reshape(16, 8, 512))
            for q in range(4):
                z = pick(y, q, 1)
                z = pltpu.roll(z, 2 * q, 1) if q else z
                for i in range(4):
                    out_ref[:, q, i, c, start : start + 8, :] = z[:, :, 128 * i : 128 * i + 128]

    def pair(c, _):
        work((c, 8), (c + 1, 0))
        return _

    work((0, 0))
    lax.fori_loop(0, 2, pair, 0)
    work((2, 8))


def forward(x, azimuth, axial):
    y = jnp.concatenate(
        (table_dot(azimuth[0], x[:128] + x[128:]), table_dot(azimuth[1], x[:128] - x[128:])), axis=0
    )
    s = y[:, :512] + y[:, 512:]
    d = y[:, :512] - y[:, 512:]
    return jnp.concatenate(
        (
            dot_table(s[:, :256] + s[:, 256:], axial[0], False),
            dot_table(s[:, :256] - s[:, 256:], axial[1], False),
            dot_table(d, axial[2], False),
        ),
        axis=1,
    )


def backward(z, axial):
    a = dot_table(z[:, :256], axial[0], True)
    b = dot_table(z[:, 256:512], axial[1], True)
    o = dot_table(z[:, 512:], axial[2], True)
    e = jnp.concatenate((a + b, a - b), axis=1)
    return e + o, e - o


def plane(recv_ref, c):
    return jnp.concatenate([recv_ref[a, :, c].reshape(256, 128) for a in range(8)], axis=1)


def put(z, axial, send_ref, group):
    for side, y in enumerate(backward(z, axial)):
        for a in range(4):
            for c in range(3):
                block = y[128 * c : 128 * c + 128, 128 * a : 128 * a + 128]
                send_ref[4 * side + a, :, 3 * group + c] = block.reshape(16, 8, 128)


def add_to(sum_ref, c, value):
    sum_ref[...] = jnp.where(c == 0, 0.0, sum_ref[...]) + value


def first_kernel(recv_ref, azimuth_ref, zero_ref, two_ref, odd_ref, out_ref, sum_ref):
    def step(c, _):
        axial = (parts(zero_ref), parts(two_ref), parts(odd_ref))
        azimuth = tuple(lay(*parts(azimuth_ref.at[p])) for p in range(2))
        y = forward(plane(recv_ref, c), azimuth, axial)
        out_ref[c] = y
        add_to(sum_ref, c, y)
        return _

    lax.fori_loop(0, 3, step, 0)


def second_kernel(
    recv_ref,
    own_ref,
    own_sum_ref,
    azimuth_ref,
    back_ref,
    zero_ref,
    two_ref,
    odd_ref,
    keep_ref,
    pass_ref,
    field_ref,
    sum_ref,
):
    def step(c, _):
        axial = (parts(zero_ref), parts(two_ref), parts(odd_ref))
        azimuth = tuple(lay(*parts(azimuth_ref.at[p])) for p in range(2))
        y = forward(plane(recv_ref, 3 + c), azimuth, axial)
        field_ref[c] = y
        add_to(sum_ref, c, y)
        return _

    lax.fori_loop(0, 3, step, 0)
    core = lax.axis_index("az") % 2

    def product(c, _):
        rhs = own_ref[c] * sum_ref[...] + field_ref[c] * own_sum_ref[...]
        side = []
        for parity in range(2):
            mine, theirs = back_ref.at[core, parity], back_ref.at[1 - core, parity]
            table = lay(*(jnp.concatenate((mine[i], theirs[i]), axis=0) for i in range(2)))
            side.append(table_dot(table, rhs[128 * parity : 128 * parity + 128]))
        upper, lower = side[0] + side[1], side[0] - side[1]
        keep_ref[c] = jnp.concatenate((upper[:64], lower[:64]), axis=0)
        pass_ref[c] = jnp.concatenate((upper[64:], lower[64:]), axis=0)
        return _

    lax.fori_loop(0, 3, product, 0)


def tangent_kernel(
    own_ref,
    own_sum_ref,
    other_ref,
    back_ref,
    zero_ref,
    two_ref,
    odd_ref,
    send_ref,
    sum_ref,
    turned_ref,
):
    core = lax.axis_index("az") % 2
    sum_ref[...] = other_ref[0] + other_ref[1] + other_ref[2]

    def step(c, _):
        rhs = own_ref[c] * sum_ref[...] + other_ref[c] * own_sum_ref[...]
        e = table_dot(lay(*parts(back_ref.at[core, 0])), rhs[:128])
        o = table_dot(lay(*parts(back_ref.at[core, 1])), rhs[128:])
        turned_ref[c] = jnp.concatenate((e + o, e - o), axis=0)
        return _

    lax.fori_loop(0, 3, step, 0)
    axial = (parts(zero_ref), parts(two_ref), parts(odd_ref))
    put(turned_ref[...].reshape(384, 1024), axial, send_ref, 0)


def join_kernel(tangent_ref, keep_ref, other_ref, zero_ref, two_ref, odd_ref, send_ref):
    send_ref[:, :, :3] = tangent_ref[...]
    z = keep_ref[...] + other_ref[...]
    put(z.reshape(384, 1024), (parts(zero_ref), parts(two_ref), parts(odd_ref)), send_ref, 1)


def gather_kernel(
    recv_ref, tangent_ref, second_ref, rate_ref, table_ref, out_ref, out2_ref, result_ref, scale_ref, sems
):
    radial = rate_ref.shape[0]
    azimuth_count, axial_count = 256, 1024
    axial = lax.axis_index("ax") * 128 + lax.broadcasted_iota(jnp.int32, (1, 128), 1)
    wave = jnp.minimum(axial, axial_count - axial).astype(F32) * axial_unit
    base = rate_ref[...] + wave * wave

    def scale(m, _):
        azimuth = lax.axis_index("az") * 16 + m
        wave_azimuth = jnp.minimum(azimuth, azimuth_count - azimuth).astype(F32)
        scale_ref[m] = 1.0 / (1.0 + viscosity * (base + wave_azimuth * wave_azimuth))
        return _

    lax.fori_loop(0, 16, scale, 0)
    outs = (out_ref, out2_ref)
    fields = (tangent_ref, second_ref)

    def give(which, c, core):
        place = (c, pl.ds(8 * core, 8))
        return pltpu.make_async_copy(
            result_ref.at[(which, *place)], outs[which].at[place], sems.at[which, c, core]
        )


    def step(c, _):
        for core in range(2):
            x = []
            for q in range(4):
                rows = [recv_ref[:, q, 2 * core + i, c] for i in range(2)]
                rows = jnp.concatenate(rows, axis=2)
                x.append(pltpu.roll(rows, 8 - 2 * q, 1) if q else rows)
            for p in range(4):
                y = table_dot(table_ref[p], pick(x, p, -1).reshape(128, 256))
                for n in range(2):
                    m = 8 * core + 2 * p + n
                    for which in range(2):
                        term = y[radial * n : radial * n + radial, 128 * which : 128 * which + 128]
                        value = (fields[which][c, m] + time_step * term) * scale_ref[m]
                        result_ref[which, c, m] = value
            for which in range(2):
                give(which, c, core).start(priority=which)
        return _

    lax.fori_loop(0, 3, step, 0)

    def finish(c, _):
        for which in range(2):
            for core in range(2):
                give(which, c, core).wait()
        return _

    lax.fori_loop(0, 3, finish, 0)


WHOLE = pl.BlockSpec(memory_space=pltpu.VMEM)
LEFT = pl.BlockSpec(memory_space=pl.ANY)


def call(kernel, shapes, *args, scratch=(), limit=24, specs=None, out_spec=WHOLE):
    out = [jax.ShapeDtypeStruct(shape, F32) for shape in shapes]
    return pl.pallas_call(
        kernel,
        out_shape=out,
        in_specs=specs or [WHOLE] * len(args),
        out_specs=[out_spec] * len(out),
        scratch_shapes=list(scratch),
        compiler_params=pltpu.CompilerParams(vmem_limit_bytes=limit * 1024 * 1024),
    )(*args)


def radial_tables(radial):
    t, b, n = np.meshgrid(np.arange(16), np.arange(4), np.arange(2), indexing="ij")
    there, back = [], []
    for p in range(4):
        j = (4 * t + (p - b) % 4).ravel()
        same = n.ravel()[:, None, None] == np.arange(2)[None, :, None]
        plain = np.where(same, radial[j][:, None, :], 0.0)
        high, low = halves(plain)
        none = np.zeros_like(low)
        rows = [np.stack(pair, axis=2).reshape(128, 256) for pair in ((high, high), (low, none))]
        there.append(np.concatenate(rows, axis=0))
        back.append(stacked(plain.reshape(128, 128).T))
    return np.stack(there), np.stack(back)


def body(saved_flow, saved_adjoint, tangent, second_adjoint, radial_rate):
    radial = radial_table(64)
    there, home_again = radial_tables(radial)
    half, quarter = np.arange(128), np.arange(256)
    azimuth = np.stack([halves(hartley_table(2 * half + p, half, 256)) for p in range(2)])
    kept = [np.array([16 * a + 8 * s + i for a in range(8) for i in range(8)]) for s in range(2)]
    back = np.stack(
        [
            np.stack([halves(hartley_table(rows, 2 * half + p, 256)) for p in range(2)])
            for rows in kept
        ]
    )
    axial = (
        halves(hartley_table(quarter, 4 * quarter, 1024)),
        halves(hartley_table(quarter, 4 * quarter + 2, 1024)),
        halves(hartley_table(np.arange(512), 2 * np.arange(512) + 1, 1024)),
    )
    rate = jnp.broadcast_to(radial_rate[:, None], (64, 128))
    pairs = [(i, i ^ 1) for i in range(16)]
    grid, rows = (256, 1024), (128, 1024)

    def swap(x):
        return lax.ppermute(x, "az", pairs)

    def whole(x):
        return lax.all_to_all(x, ("ax", "az"), 0, 0, tiled=True)

    (spread,) = call(
        spread_kernel,
        [(16, 4, 4, 3, 16, 128)],
        *(
            pltpu.with_memory_space_constraint(x, pltpu.HBM)
            for x in (saved_flow, tangent, second_adjoint, saved_adjoint)
        ),
        pltpu.with_memory_space_constraint(jnp.asarray(there), pltpu.HBM),
        scratch=(
            pltpu.VMEM((4, 256, 256), BF16),
            pltpu.VMEM((4, 3, 16, 64, 128), F32),
            pltpu.SemaphoreType.DMA,
            pltpu.SemaphoreType.DMA((4, 3, 2)),
        ),
        specs=[LEFT] * 5,
    )
    recv = whole(spread.reshape(128, 6, 16, 128)).reshape(8, 16, 6, 16, 128)
    own, own_sum = call(first_kernel, [(3, *grid), grid], recv, azimuth, *axial)
    other = swap(own)
    keep, passed = call(
        second_kernel,
        [(3, *rows)] * 2,
        recv,
        own,
        own_sum,
        azimuth,
        back,
        *axial,
        scratch=(pltpu.VMEM((3, *grid), F32), pltpu.VMEM(grid, F32)),
    )
    joined = swap(passed)
    (turned,) = call(
        tangent_kernel,
        [(8, 16, 3, 8, 128)],
        own,
        own_sum,
        other,
        back,
        *axial,
        scratch=(pltpu.VMEM(grid, F32), pltpu.VMEM((3, *rows), F32)),
    )
    (send,) = call(join_kernel, [(8, 16, 6, 8, 128)], turned, keep, joined, *axial)
    home = whole(send.reshape(128, 6, 8, 128)).reshape(16, 4, 4, 3, 8, 128)
    shape = tangent.shape
    return tuple(
        call(
            gather_kernel,
            [shape, shape],
            home,
            tangent,
            second_adjoint,
            rate,
            home_again,
            scratch=(
                pltpu.VMEM((2, *shape), F32),
                pltpu.VMEM(shape[1:], F32),
                pltpu.SemaphoreType.DMA((2, 3, 2)),
            ),
            out_spec=LEFT,
        )
    )


def solution(mesh):
    spec = P(None, "az", None, "ax")
    return jax.shard_map(
        body, mesh=mesh, in_specs=(spec,) * 4 + (P(),), out_specs=(spec, spec), check_vma=False
    )
```

```python
import math

import jax
import jax.numpy as jnp
import numpy as np
from jax import lax
from jax.experimental import pallas as pl
from jax.experimental.pallas import tpu as pltpu
from jax.sharding import PartitionSpec as P

time_step = 0.1
viscosity = 0.005
axial_unit = 2.0 * math.pi / 20.0
F32 = jnp.float32
BF16 = jnp.bfloat16


def radial_table(count):
    points = np.arange(count)[:, None]
    orders = np.arange(count)[None, :]
    phases = orders * (2 * points + 1) % (4 * count)
    scales = np.where(orders == 0, math.sqrt(1.0 / count), math.sqrt(2.0 / count))
    return np.cos(phases * (math.pi / (2.0 * count))) * scales


def hartley_table(rows, cols, length):
    angles = (rows[:, None] * cols[None, :] % length) * (2.0 * math.pi / length)
    return (np.cos(angles) + np.sin(angles)) / math.sqrt(length)


def halves(table):
    table = np.asarray(table, np.float32)
    high = table.astype(BF16)
    low = (table - high.astype(np.float32)).astype(BF16)
    return np.stack((high, low))


def split(x):
    high = x.astype(BF16)
    return high, (x - high.astype(F32)).astype(BF16)


def stacked(table):
    high, low = halves(table)
    return np.block([[high, high], [low, np.zeros_like(low)]])


def lay(high, low):
    right = jnp.concatenate((high, jnp.zeros_like(low)), axis=0)
    return jnp.concatenate((jnp.concatenate((high, low), axis=0), right), axis=1)


def table_dot(table, x):
    out = jnp.dot(table, jnp.concatenate(split(x), axis=0), preferred_element_type=F32)
    half = out.shape[0] // 2
    return out[:half] + out[half:]


def dot_table(x, table, turned):
    high, low = split(x)
    numbers = (((1,), (1 if turned else 0,)), ((), ()))
    both = lax.dot_general(
        jnp.concatenate((high, low), axis=0), table[0], numbers, preferred_element_type=F32
    )
    rest = lax.dot_general(high, table[1], numbers, preferred_element_type=F32)
    return both[: x.shape[0]] + both[x.shape[0] :] + rest


def parts(ref):
    return ref[0], ref[1]


def pick(arrays, first, step):
    block = lax.broadcasted_iota(jnp.int32, arrays[0].shape, 1) // 2
    out = arrays[first % 4]
    for b in range(1, 4):
        out = jnp.where(block == b, arrays[(first + step * b) % 4], out)
    return out


def spread_kernel(
    flow_ref,
    tangent_ref,
    second_ref,
    adjoint_ref,
    radial_ref,
    out_ref,
    compact_ref,
    table_ref,
    field_ref,
    sem,
    sems,
):
    fetch_table = pltpu.make_async_copy(radial_ref, compact_ref, sem)

    def fetch(i, ref, c, start):
        place = (c, pl.ds(start, 8))
        return pltpu.make_async_copy(
            ref.at[place], field_ref.at[(i, *place)], sems.at[i, c, start // 8]
        )

    fields = tuple(enumerate((flow_ref, second_ref, tangent_ref, adjoint_ref)))
    for c in range(3):
        for start in (0, 8):
            for i, ref in fields:
                fetch(i, ref, c, start).start(priority=i % 2)
            if c == start == 0:
                fetch_table.start()
    fetch_table.wait()
    odd = lax.broadcasted_iota(jnp.int32, (128, 128), 0) % 2
    for p in range(4):
        for i in range(2):
            part = compact_ref[p, i].astype(F32)
            for n in range(2):
                rows, lanes = slice(128 * i, 128 * i + 128), slice(128 * n, 128 * n + 128)
                table_ref[p, rows, lanes] = jnp.where(odd == n, part, 0.0).astype(BF16)

    def work(*groups):
        for place in groups:
            for i, ref in fields:
                fetch(i, ref, *place).wait()
        for c, start in groups:
            y = []
            for p in range(4):
                x = []
                for m in (start + 2 * p, start + 2 * p + 1):
                    x.extend(split(jnp.concatenate([field_ref[i, c, m] for i in range(4)], axis=1)))
                out = jnp.dot(
                    table_ref[p], jnp.concatenate(x, axis=0), preferred_element_type=F32
                )
                y.append((out[:128] + out[128:]).reshape(16, 8, 512))
            for q in range(4):
                z = pick(y, q, 1)
                z = pltpu.roll(z, 2 * q, 1) if q else z
                for i in range(4):
                    out_ref[:, q, i, c, start : start + 8, :] = z[:, :, 128 * i : 128 * i + 128]

    def pair(c, _):
        work((c, 8), (c + 1, 0))
        return _

    work((0, 0))
    lax.fori_loop(0, 2, pair, 0)
    work((2, 8))


def forward(x, azimuth, axial):
    y = jnp.concatenate(
        (table_dot(azimuth[0], x[:128] + x[128:]), table_dot(azimuth[1], x[:128] - x[128:])), axis=0
    )
    s = y[:, :512] + y[:, 512:]
    d = y[:, :512] - y[:, 512:]
    return jnp.concatenate(
        (
            dot_table(s[:, :256] + s[:, 256:], axial[0], False),
            dot_table(s[:, :256] - s[:, 256:], axial[1], False),
            dot_table(d, axial[2], False),
        ),
        axis=1,
    )


def backward(z, axial):
    a = dot_table(z[:, :256], axial[0], True)
    b = dot_table(z[:, 256:512], axial[1], True)
    o = dot_table(z[:, 512:], axial[2], True)
    e = jnp.concatenate((a + b, a - b), axis=1)
    return e + o, e - o


def plane(recv_ref, c):
    return jnp.concatenate([recv_ref[a, :, c].reshape(256, 128) for a in range(8)], axis=1)


def put(z, axial, send_ref, group):
    for side, y in enumerate(backward(z, axial)):
        for a in range(4):
            for c in range(3):
                block = y[128 * c : 128 * c + 128, 128 * a : 128 * a + 128]
                send_ref[4 * side + a, :, 3 * group + c] = block.reshape(16, 8, 128)


def add_to(sum_ref, c, value):
    sum_ref[...] = jnp.where(c == 0, 0.0, sum_ref[...]) + value


def first_kernel(recv_ref, azimuth_ref, zero_ref, two_ref, odd_ref, out_ref, sum_ref):
    def step(c, _):
        axial = (parts(zero_ref), parts(two_ref), parts(odd_ref))
        azimuth = tuple(lay(*parts(azimuth_ref.at[p])) for p in range(2))
        y = forward(plane(recv_ref, c), azimuth, axial)
        out_ref[c] = y
        add_to(sum_ref, c, y)
        return _

    lax.fori_loop(0, 3, step, 0)


def second_kernel(
    recv_ref,
    own_ref,
    own_sum_ref,
    azimuth_ref,
    back_ref,
    zero_ref,
    two_ref,
    odd_ref,
    keep_ref,
    pass_ref,
    field_ref,
    sum_ref,
):
    def step(c, _):
        axial = (parts(zero_ref), parts(two_ref), parts(odd_ref))
        azimuth = tuple(lay(*parts(azimuth_ref.at[p])) for p in range(2))
        y = forward(plane(recv_ref, 3 + c), azimuth, axial)
        field_ref[c] = y
        add_to(sum_ref, c, y)
        return _

    lax.fori_loop(0, 3, step, 0)
    core = lax.axis_index("az") % 2

    def product(c, _):
        rhs = own_ref[c] * sum_ref[...] + field_ref[c] * own_sum_ref[...]
        side = []
        for parity in range(2):
            mine, theirs = back_ref.at[core, parity], back_ref.at[1 - core, parity]
            table = lay(*(jnp.concatenate((mine[i], theirs[i]), axis=0) for i in range(2)))
            side.append(table_dot(table, rhs[128 * parity : 128 * parity + 128]))
        upper, lower = side[0] + side[1], side[0] - side[1]
        keep_ref[c] = jnp.concatenate((upper[:64], lower[:64]), axis=0)
        pass_ref[c] = jnp.concatenate((upper[64:], lower[64:]), axis=0)
        return _

    lax.fori_loop(0, 3, product, 0)


def tangent_kernel(
    own_ref,
    own_sum_ref,
    other_ref,
    back_ref,
    zero_ref,
    two_ref,
    odd_ref,
    send_ref,
    sum_ref,
    turned_ref,
):
    core = lax.axis_index("az") % 2
    sum_ref[...] = other_ref[0] + other_ref[1] + other_ref[2]

    def step(c, _):
        rhs = own_ref[c] * sum_ref[...] + other_ref[c] * own_sum_ref[...]
        e = table_dot(lay(*parts(back_ref.at[core, 0])), rhs[:128])
        o = table_dot(lay(*parts(back_ref.at[core, 1])), rhs[128:])
        turned_ref[c] = jnp.concatenate((e + o, e - o), axis=0)
        return _

    lax.fori_loop(0, 3, step, 0)
    axial = (parts(zero_ref), parts(two_ref), parts(odd_ref))
    put(turned_ref[...].reshape(384, 1024), axial, send_ref, 0)


def join_kernel(tangent_ref, keep_ref, other_ref, zero_ref, two_ref, odd_ref, send_ref):
    send_ref[:, :, :3] = tangent_ref[...]
    z = keep_ref[...] + other_ref[...]
    put(z.reshape(384, 1024), (parts(zero_ref), parts(two_ref), parts(odd_ref)), send_ref, 1)


def gather_kernel(
    recv_ref, tangent_ref, second_ref, rate_ref, table_ref, out_ref, out2_ref, result_ref, scale_ref, sems
):
    radial = rate_ref.shape[0]
    azimuth_count, axial_count = 256, 1024
    axial = lax.axis_index("ax") * 128 + lax.broadcasted_iota(jnp.int32, (1, 128), 1)
    wave = jnp.minimum(axial, axial_count - axial).astype(F32) * axial_unit
    base = rate_ref[...] + wave * wave

    def scale(m, _):
        azimuth = lax.axis_index("az") * 16 + m
        wave_azimuth = jnp.minimum(azimuth, azimuth_count - azimuth).astype(F32)
        scale_ref[m] = 1.0 / (1.0 + viscosity * (base + wave_azimuth * wave_azimuth))
        return _

    lax.fori_loop(0, 16, scale, 0)
    outs = (out_ref, out2_ref)
    fields = (tangent_ref, second_ref)

    def give(which, c, core):
        place = (c, pl.ds(8 * core, 8))
        return pltpu.make_async_copy(
            result_ref.at[(which, *place)], outs[which].at[place], sems.at[which, c, core]
        )


    def step(c, _):
        for core in range(2):
            x = []
            for q in range(4):
                rows = [recv_ref[:, q, 2 * core + i, c] for i in range(2)]
                rows = jnp.concatenate(rows, axis=2)
                x.append(pltpu.roll(rows, 8 - 2 * q, 1) if q else rows)
            for p in range(4):
                y = table_dot(table_ref[p], pick(x, p, -1).reshape(128, 256))
                for n in range(2):
                    m = 8 * core + 2 * p + n
                    for which in range(2):
                        term = y[radial * n : radial * n + radial, 128 * which : 128 * which + 128]
                        value = (fields[which][c, m] + time_step * term) * scale_ref[m]
                        result_ref[which, c, m] = value
            for which in range(2):
                give(which, c, core).start(priority=which)
        return _

    lax.fori_loop(0, 3, step, 0)

    def finish(c, _):
        for which in range(2):
            for core in range(2):
                give(which, c, core).wait()
        return _

    lax.fori_loop(0, 3, finish, 0)


WHOLE = pl.BlockSpec(memory_space=pltpu.VMEM)
LEFT = pl.BlockSpec(memory_space=pl.ANY)


def call(kernel, shapes, *args, scratch=(), limit=24, specs=None, out_spec=WHOLE):
    out = [jax.ShapeDtypeStruct(shape, F32) for shape in shapes]
    return pl.pallas_call(
        kernel,
        out_shape=out,
        in_specs=specs or [WHOLE] * len(args),
        out_specs=[out_spec] * len(out),
        scratch_shapes=list(scratch),
        compiler_params=pltpu.CompilerParams(vmem_limit_bytes=limit * 1024 * 1024),
    )(*args)


def radial_tables(radial):
    t, b, n = np.meshgrid(np.arange(16), np.arange(4), np.arange(2), indexing="ij")
    there, back = [], []
    for p in range(4):
        j = (4 * t + (p - b) % 4).ravel()
        same = n.ravel()[:, None, None] == np.arange(2)[None, :, None]
        plain = np.where(same, radial[j][:, None, :], 0.0)
        high, low = halves(radial[j])
        none = np.zeros_like(low)
        there.append(np.stack([np.concatenate(x, axis=1) for x in ((high, high), (low, none))]))
        back.append(stacked(plain.reshape(128, 128).T))
    return np.stack(there), np.stack(back)


def body(saved_flow, saved_adjoint, tangent, second_adjoint, radial_rate):
    radial = radial_table(64)
    there, home_again = radial_tables(radial)
    half, quarter = np.arange(128), np.arange(256)
    azimuth = np.stack([halves(hartley_table(2 * half + p, half, 256)) for p in range(2)])
    kept = [np.array([16 * a + 8 * s + i for a in range(8) for i in range(8)]) for s in range(2)]
    back = np.stack(
        [
            np.stack([halves(hartley_table(rows, 2 * half + p, 256)) for p in range(2)])
            for rows in kept
        ]
    )
    axial = (
        halves(hartley_table(quarter, 4 * quarter, 1024)),
        halves(hartley_table(quarter, 4 * quarter + 2, 1024)),
        halves(hartley_table(np.arange(512), 2 * np.arange(512) + 1, 1024)),
    )
    rate = jnp.broadcast_to(radial_rate[:, None], (64, 128))
    pairs = [(i, i ^ 1) for i in range(16)]
    grid, rows = (256, 1024), (128, 1024)

    def swap(x):
        return lax.ppermute(x, "az", pairs)

    def whole(x):
        return lax.all_to_all(x, ("ax", "az"), 0, 0, tiled=True)

    (spread,) = call(
        spread_kernel,
        [(16, 4, 4, 3, 16, 128)],
        *(
            pltpu.with_memory_space_constraint(x, pltpu.HBM)
            for x in (saved_flow, tangent, second_adjoint, saved_adjoint)
        ),
        pltpu.with_memory_space_constraint(jnp.asarray(there), pltpu.HBM),
        scratch=(
            pltpu.VMEM((4, 2, 128, 128), BF16),
            pltpu.VMEM((4, 256, 256), BF16),
            pltpu.VMEM((4, 3, 16, 64, 128), F32),
            pltpu.SemaphoreType.DMA,
            pltpu.SemaphoreType.DMA((4, 3, 2)),
        ),
        specs=[LEFT] * 5,
    )
    recv = whole(spread.reshape(128, 6, 16, 128)).reshape(8, 16, 6, 16, 128)
    own, own_sum = call(first_kernel, [(3, *grid), grid], recv, azimuth, *axial)
    other = swap(own)
    keep, passed = call(
        second_kernel,
        [(3, *rows)] * 2,
        recv,
        own,
        own_sum,
        azimuth,
        back,
        *axial,
        scratch=(pltpu.VMEM((3, *grid), F32), pltpu.VMEM(grid, F32)),
    )
    joined = swap(passed)
    (turned,) = call(
        tangent_kernel,
        [(8, 16, 3, 8, 128)],
        own,
        own_sum,
        other,
        back,
        *axial,
        scratch=(pltpu.VMEM(grid, F32), pltpu.VMEM((3, *rows), F32)),
    )
    (send,) = call(join_kernel, [(8, 16, 6, 8, 128)], turned, keep, joined, *axial)
    home = whole(send.reshape(128, 6, 8, 128)).reshape(16, 4, 4, 3, 8, 128)
    shape = tangent.shape
    return tuple(
        call(
            gather_kernel,
            [shape, shape],
            home,
            tangent,
            second_adjoint,
            rate,
            home_again,
            scratch=(
                pltpu.VMEM((2, *shape), F32),
                pltpu.VMEM(shape[1:], F32),
                pltpu.SemaphoreType.DMA((2, 3, 2)),
            ),
            out_spec=LEFT,
        )
    )


def solution(mesh):
    spec = P(None, "az", None, "ax")
    return jax.shard_map(
        body, mesh=mesh, in_specs=(spec,) * 4 + (P(),), out_specs=(spec, spec), check_vma=False
    )
```
